32 devices in a mesh: parts: 2 (over y), dp: 8 (over z, x), tensor: 2 (over core).
Axes of the slice: x: 2, y: 2, z: 4, core: 2. Of those that a mesh axis runs over, the one named last changes fastest.
Arguments:
- acoustic: bfloat16 [3072, 4096], P(('parts', 'dp'), 'tensor'), parts along dimension 0, may hold values from -6 to 6
- norm_gain: float32 [4096], replicated, may hold values from 0.1 to 1.9
- up_weight: bfloat16 [64, 32, 16384], P('tensor', None, 'dp'), may hold values from -0.25 to 0.25
- down_weight: bfloat16 [64, 32, 16384], P('tensor', None, 'dp'), may hold values from -0.1875 to 0.1875
- up_keep: int32 [64, 64, 32], P(None, 'tensor'), may hold values from 0 to 1, as said below
- down_keep: int32 [64, 64, 32], P(None, 'tensor'), may hold values from 0 to 1, as said below
- language: int32 [16], P(('parts', 'dp')), parts along dimension 0, may hold values from 0 to 63
- lengths: int32 [16], P(('parts', 'dp')), parts along dimension 0, may hold values from 48 to 192, as said below
Outputs:
- encoded: bfloat16 [3072, 4096], P(('parts', 'dp'), 'tensor'), parts along dimension 0
The draws below stay inside these ranges and needn't reach their ends.
There are 2 independent parts, one for each index of `parts`. The reference program is written for one: setup_inputs(seed, part) draws one part's arguments, and reference() takes and returns one part's arrays. A program takes and returns all parts, laid end to end along the dimension named above; an argument that names none is the same for every part. Nothing has to cross between parts.
Inputs may be any that keep to these rules, and one draw needn't show every extreme that they name: `up_keep`: for every language and hidden block, exactly one feature block of each aligned run of 8 (blocks k * 8 to k * 8 + 7) is kept (1), the others are 0. `down_keep`: for every language and hidden block, exactly one feature block of each aligned run of 8 is kept (1), the others are 0. `lengths`: some utterance is full in every draw.
All inputs are finite; a program needn't handle non-finite values.
Results may differ from the reference program's by a relative error of at most 0.006.
Values may be sent and summed in bfloat16 or wider, within the bound.
No kernel may reach another device: no remote copies, remote signals or barrier semaphores. Data moves between devices by JAX's collectives and lax.ppermute only.
A program may use at most 128 MiB of HBM per device.

```python
import math
import jax
import jax.numpy as jnp
import numpy as np
from jax import lax

D = 4096
FF = 8192
BLK = 128
GROUP = 8
LANGS = 64
FRAMES = 192
DB = 32
HB = 64
UTTS = 8
TOKENS = 1536
N_TENSOR = 2


def keep_draw(key):
    runs = D // (BLK * GROUP)
    chosen = jax.random.randint(key, (LANGS, FF // BLK, runs), 0, GROUP)
    onehot = (chosen[..., None] == jnp.arange(GROUP, dtype=jnp.int32)).astype(jnp.int32)
    return onehot.reshape(LANGS, FF // BLK, D // BLK)


def draw_up_keep(key, part):
    return keep_draw(jax.random.fold_in(key, 11))


def draw_down_keep(key, part):
    return keep_draw(jax.random.fold_in(key, 23))


def draw_lengths(key, part):
    first = jax.random.fold_in(key, 37)
    second = jax.random.fold_in(key, 41)
    drawn = jax.random.randint(first, (UTTS,), FRAMES // 4, FRAMES + 1)
    fullest = jax.random.randint(second, (), 0, UTTS)
    return jnp.where(jnp.arange(UTTS) == fullest, FRAMES, drawn).astype(jnp.int32)


def with_ends(result, rng, least, largest):
    longest = result.shape.index(max(result.shape))
    spots = []
    for shift in (0, 1):
        where = [jax.random.randint(jax.random.fold_in(rng, axis), (), 0, length) for axis, length in enumerate(result.shape)]
        where[longest] = (where[longest] + shift) % result.shape[longest]
        spots.append(tuple(where))
    return result.at[spots[0]].set(least).at[spots[1]].set(largest)


def level_of(own_key, shape, split, smallest, top_value):
    factor_of, own = 1.0, jax.random.fold_in(own_key, 6)
    for dim, blocks in split:
        heights = jnp.exp(jax.random.uniform(jax.random.fold_in(own, dim), (blocks,), jnp.float32, smallest / len(split), top_value / len(split)))
        factor_of = factor_of * jnp.repeat(heights, shape[dim] // blocks).reshape([-1 if axis == dim else 1 for axis in range(len(shape))])
    return factor_of


def rank_table(count, skew):
    weights = [(1 << 20) // math.isqrt(rank ** skew) + 1 for rank in range(1, count + 1)]
    spread = 1 + sum(weights) // (1 << 30)
    return np.cumsum(np.array([max(1, weight // spread) for weight in weights]))


def skewed_ids(key, shape, number_of, lean):
    listing = rank_table(number_of, lean)
    pick = jax.random.randint(jax.random.fold_in(key, 1), shape, 0, int(listing[number_of - 1]))
    grade = jnp.searchsorted(jnp.asarray(listing, jnp.int32), pick, side="right")
    return jax.random.permutation(jax.random.fold_in(key, 2), number_of)[grade].astype(jnp.int32)


def normal_values(stream_key, extent, deviation, bound, pieces=(), held_as=jnp.bfloat16):
    array = jax.random.normal(stream_key, extent, jnp.float32) * deviation
    if len(pieces) > 0:
        array = level_of(stream_key, extent, pieces, -0.22, 0.18) * array
    return jnp.clip(array, min=-bound, max=bound).astype(held_as)


def setup_inputs(seed: int = 0, part: int = 0) -> dict:
    key_list = jax.random.split(jax.random.key(seed), 9)
    part_keys = jax.random.split(jax.random.fold_in(key_list[8], part), 9)
    return {
        "acoustic": normal_values(part_keys[0], (TOKENS, D), 1.0, 6.0, ((0, 8), (1, 2))),
        "norm_gain": jnp.clip(1.0 + 0.18 * jax.random.normal(key_list[1], (D,), jnp.float32), 0.1, 1.9),
        "up_weight": normal_values(key_list[2], (HB, DB, BLK * BLK), (D // GROUP) ** -0.5, 0.25, ((0, 2), (2, 8))),
        "down_weight": normal_values(key_list[3], (HB, DB, BLK * BLK), (FF // GROUP) ** -0.5, 0.1875, ((0, 2), (2, 8))),
        "up_keep": draw_up_keep(jax.random.fold_in(key_list[8], 71), part),
        "down_keep": draw_down_keep(jax.random.fold_in(key_list[8], 71), part),
        "language": with_ends(skewed_ids(part_keys[6], (UTTS,), LANGS, 2), jax.random.fold_in(part_keys[6], 3), 0, LANGS - 1).astype(jnp.int32),
        "lengths": draw_lengths(jax.random.fold_in(jax.random.fold_in(key_list[8], part), 71), part),
    }


def kept_index(keep_mask):
    hidden_blocks = keep_mask.shape[1]
    runs = keep_mask.shape[2] // GROUP
    picks = jnp.arange(GROUP, dtype=jnp.int32)
    within = lax.optimization_barrier(jnp.sum(keep_mask.reshape(LANGS, hidden_blocks, runs, GROUP) * picks, axis=-1))
    return (within + jnp.arange(runs, dtype=jnp.int32) * GROUP).astype(jnp.int32)

def reference(acoustic, norm_gain, up_weight, down_weight, up_keep, down_keep, language, lengths):
    hidden_blocks = FF // BLK
    feat_blocks = D // BLK
    half = hidden_blocks // N_TENSOR
    up_blocks4 = up_weight.reshape(hidden_blocks, feat_blocks, BLK, BLK)
    down_blocks4 = down_weight.reshape(hidden_blocks, feat_blocks, BLK, BLK)
    up_index = kept_index(up_keep)
    down_index = kept_index(down_keep)
    widened = acoustic.astype(jnp.float32)
    scale = lax.rsqrt(lax.optimization_barrier(jnp.mean(widened * widened, axis=-1, keepdims=True)) + 1e-06)
    normed = (widened * scale * norm_gain).astype(jnp.bfloat16)
    row_index = jnp.arange(hidden_blocks, dtype=jnp.int32)[:, None]
    block_ids = jnp.arange(feat_blocks, dtype=jnp.int32)

    def one_utterance(pair):
        frames_in, lang = pair
        up_sel = up_index[lang]
        down_sel = down_index[lang]
        chosen = frames_in.reshape(FRAMES, feat_blocks, BLK)[:, up_sel].astype(jnp.float32)
        weights_up = up_blocks4[row_index, up_sel].astype(jnp.float32)
        before = jnp.einsum('thgi,hgij->thj', chosen, weights_up)
        active = lax.optimization_barrier(jax.nn.silu(before).astype(jnp.bfloat16)).astype(jnp.float32)
        weights_down = down_blocks4[row_index, down_sel].astype(jnp.float32)
        onehot = (down_sel[:, :, None] == block_ids).astype(jnp.float32)
        total = jnp.zeros((FRAMES, D), jnp.float32)
        for part_at in range(N_TENSOR):
            lower = part_at * half
            contrib = jnp.einsum('thi,hgij->thgj', active[:, lower:lower + half], weights_down[lower:lower + half])
            summed = jnp.einsum('thgj,hgd->tdj', contrib, onehot[lower:lower + half], precision=lax.Precision.HIGHEST)
            rounded = lax.optimization_barrier(summed.reshape(FRAMES, D).astype(jnp.bfloat16))
            total = total + rounded.astype(jnp.float32)
        return total
    feedfwd = lax.map(one_utterance, (normed.reshape(UTTS, FRAMES, D), language)).reshape(UTTS * FRAMES, D)
    valid = (jnp.arange(FRAMES, dtype=jnp.int32)[None, :] < lengths[:, None]).reshape(UTTS * FRAMES)
    return ((widened + feedfwd) * valid[:, None].astype(jnp.float32)).astype(jnp.bfloat16)
```

```python
import functools

import jax
import jax.numpy as jnp
from jax import lax
from jax.experimental import pallas as pl
from jax.experimental.pallas import tpu as pltpu
from jax.sharding import PartitionSpec as P

BLK = 128
GROUP = 8
HSTEP = 4


def kept_within(keep_mask):
    nlangs, hidden_blocks, feat_blocks = keep_mask.shape
    runs = feat_blocks // GROUP
    picks = jnp.arange(GROUP, dtype=jnp.int32)
    return jnp.sum(keep_mask.reshape(nlangs, hidden_blocks, runs, GROUP) * picks, axis=-1)


def kept_index(keep_mask):
    within = kept_within(keep_mask)
    return within + jnp.arange(within.shape[-1], dtype=jnp.int32) * GROUP


def pick_kernel(which, wanted, weight_ref, *refs, rows, runs):
    out_refs, spread = refs[:-1], refs[-1]
    step = pl.program_id(0)
    for h in range(HSTEP):
        for row in range(rows):
            tile = weight_ref[h, :, row * BLK:(row + 1) * BLK].astype(jnp.float32)
            for g in range(runs):
                spread[h * runs + g, row * GROUP:(row + 1) * GROUP, :] = tile[g * GROUP:(g + 1) * GROUP]
    for u, out_ref in enumerate(out_refs):
        for h in range(HSTEP):
            for g in range(runs):
                at = wanted[u, (step * HSTEP + h) * runs + g]
                block = spread[h * runs + g, pl.ds(at, rows, stride=GROUP), :]
                out_ref[h, g] = block.astype(jnp.bfloat16)


def pick_blocks(weight, wanted, which, runs):
    hidden_blocks, _, width = weight.shape
    rows = width // BLK
    utts = wanted.shape[0]
    out_shape = jax.ShapeDtypeStruct((hidden_blocks, runs, rows, BLK), jnp.bfloat16)
    out_spec = pl.BlockSpec((HSTEP, runs, rows, BLK), lambda i, *_: (i, 0, 0, 0))
    return pl.pallas_call(
        functools.partial(pick_kernel, rows=rows, runs=runs),
        grid_spec=pltpu.PrefetchScalarGridSpec(
            num_scalar_prefetch=2,
            grid=(hidden_blocks // HSTEP,),
            in_specs=[pl.BlockSpec((HSTEP, runs * GROUP, width), lambda i, which, wanted: (i, which[0], 0))],
            out_specs=[out_spec] * utts,
            scratch_shapes=[pltpu.VMEM((HSTEP * runs, rows * GROUP, BLK), jnp.float32)],
        ),
        out_shape=[out_shape] * utts,
        name="pick_blocks",
    )(which, wanted, weight)


def fill_weights(held, weight_refs, owner, h, runs, rows):
    for k, ref in enumerate(weight_refs):
        start = pl.multiple_of(owner[k] * rows, rows)
        for g in range(runs):
            held[g, pl.ds(start, rows), :] = ref[h, g]


def up_kernel(owner, slots, normed_ref, *refs, runs, rows):
    weight_refs, active_ref, held = refs[:-2], refs[-2], refs[-1]
    step = pl.program_id(0)
    for h in range(HSTEP):
        fill_weights(held.at[h], weight_refs, owner, h, runs, rows)
    for h in range(HSTEP):
        before = None
        for g in range(runs):
            slot = slots[(step * HSTEP + h) * runs + g]
            term = jnp.dot(normed_ref[slot], held[h, g], preferred_element_type=jnp.float32)
            before = term if before is None else before + term
        active_ref[h] = (before / (1.0 + jnp.exp(-before))).astype(jnp.bfloat16)


def up_project(owner, slots, normed, weights):
    hidden_blocks, runs, rows, _ = weights[0].shape
    slots_all, frames, _ = normed.shape
    return pl.pallas_call(
        functools.partial(up_kernel, runs=runs, rows=rows),
        grid_spec=pltpu.PrefetchScalarGridSpec(
            num_scalar_prefetch=2,
            grid=(hidden_blocks // HSTEP,),
            in_specs=[pl.BlockSpec((slots_all, frames, BLK), lambda i, *_: (0, 0, 0))]
            + [pl.BlockSpec((HSTEP, runs, rows, BLK), lambda i, *_: (i, 0, 0, 0))] * len(weights),
            out_specs=pl.BlockSpec((HSTEP, frames, BLK), lambda i, *_: (i, 0, 0)),
            scratch_shapes=[pltpu.VMEM((HSTEP, runs, BLK, BLK), jnp.bfloat16)],
        ),
        out_shape=jax.ShapeDtypeStruct((hidden_blocks, frames, BLK), jnp.bfloat16),
        name="up_project",
    )(owner, slots, normed, *weights)


def down_steps(owner, wanted, active_ref, weight_refs, held, total, runs, rows):
    step = pl.program_id(0)

    @pl.when(step == 0)
    def _():
        total[...] = jnp.zeros_like(total)

    for h in range(HSTEP):
        fill_weights(held.at[h], weight_refs, owner, h, runs, rows)
    for h in range(HSTEP):
        for g in range(runs):
            at = g * GROUP + wanted[(step * HSTEP + h) * runs + g]
            total[at] += jnp.dot(active_ref[h], held[h, g], preferred_element_type=jnp.float32)


def down_other_kernel(owner, wanted, active_ref, *refs, runs, rows):
    weight_refs, out_ref, held, total = refs[:-3], refs[-3], refs[-2], refs[-1]
    down_steps(owner, wanted, active_ref, weight_refs, held, total, runs, rows)

    @pl.when(pl.program_id(0) == pl.num_programs(0) - 1)
    def _():
        out_ref[...] = total[...].astype(jnp.bfloat16)


def down_own_kernel(owner, wanted, length, active_ref, acoustic_ref, peer_ref, *refs, runs, rows):
    weight_refs, out_ref, held, total = refs[:-3], refs[-3], refs[-2], refs[-1]
    down_steps(owner, wanted, active_ref, weight_refs, held, total, runs, rows)

    @pl.when(pl.program_id(0) == pl.num_programs(0) - 1)
    def _():
        frames = out_ref.shape[0]
        valid = lax.broadcasted_iota(jnp.int32, (frames, BLK), 0) < length[0]
        for d in range(runs * GROUP):
            lanes = slice(d * BLK, (d + 1) * BLK)
            feedfwd = total[d].astype(jnp.bfloat16).astype(jnp.float32) + peer_ref[d].astype(jnp.float32)
            summed = acoustic_ref[:, lanes].astype(jnp.float32) + feedfwd
            out_ref[:, lanes] = jnp.where(valid, summed, 0.0).astype(jnp.bfloat16)


def down_project(owner, wanted, active, weights, final=None):
    hidden_blocks, runs, rows, _ = weights[0].shape
    frames = active.shape[1]
    outs = runs * GROUP
    in_specs = [pl.BlockSpec((HSTEP, frames, BLK), lambda i, *_: (i, 0, 0))]
    weight_specs = [pl.BlockSpec((HSTEP, runs, rows, BLK), lambda i, *_: (i, 0, 0, 0))] * len(weights)
    scratch = [pltpu.VMEM((HSTEP, runs, BLK, BLK), jnp.bfloat16), pltpu.VMEM((outs, frames, BLK), jnp.float32)]
    if final is None:
        return pl.pallas_call(
            functools.partial(down_other_kernel, runs=runs, rows=rows),
            grid_spec=pltpu.PrefetchScalarGridSpec(
                num_scalar_prefetch=2,
                grid=(hidden_blocks // HSTEP,),
                in_specs=in_specs + weight_specs,
                out_specs=pl.BlockSpec((outs, frames, BLK), lambda i, *_: (0, 0, 0)),
                scratch_shapes=scratch,
            ),
            out_shape=jax.ShapeDtypeStruct((outs, frames, BLK), jnp.bfloat16),
            name="down_other",
        )(owner, wanted, active, *weights)
    lengths, acoustic, peer = final
    in_specs += [
        pl.BlockSpec((frames, outs * BLK), lambda i, *_: (0, 0)),
        pl.BlockSpec((outs, frames, BLK), lambda i, *_: (0, 0, 0)),
    ]
    return pl.pallas_call(
        functools.partial(down_own_kernel, runs=runs, rows=rows),
        grid_spec=pltpu.PrefetchScalarGridSpec(
            num_scalar_prefetch=3,
            grid=(hidden_blocks // HSTEP,),
            in_specs=in_specs + weight_specs,
            out_specs=pl.BlockSpec((frames, outs * BLK), lambda i, *_: (0, 0)),
            scratch_shapes=scratch,
        ),
        out_shape=jax.ShapeDtypeStruct((frames, outs * BLK), jnp.bfloat16),
        name="down_own",
    )(owner, wanted, lengths, active, acoustic, peer, *weights)


def swap(value, axis, size, step):
    return lax.ppermute(value, axis, [(i, i ^ step) for i in range(size)])


def split_body(acoustic, norm_gain, up_weight, down_weight, up_keep, down_keep, language, lengths, *, dp):
    frames, features = acoustic.shape
    nlangs, hidden_blocks, feat_blocks = up_keep.shape
    runs = feat_blocks // GROUP
    own_runs = runs // 2
    here = lax.axis_index("dp").astype(jnp.int32)
    core = lax.axis_index("tensor").astype(jnp.int32)
    order = list(range(dp // 2, dp)) + list(range(1, dp // 2))
    heard = {k: swap(language, "dp", dp, k) for k in order}
    heard[0] = language
    far = order[:dp // 2]
    near = order[dp // 2:] + [0]
    up_table = kept_within(up_keep)
    down_table = kept_within(down_keep)
    core_first = jnp.where(
        core == 0, down_table, jnp.concatenate([down_table[..., own_runs:], down_table[..., :own_runs]], axis=-1)
    )

    def wanted_of(peers, table):
        langs = jnp.concatenate([heard[k] for k in peers])
        chooser = (langs[:, None] == jnp.arange(nlangs, dtype=jnp.int32)).astype(jnp.int32)
        return jnp.einsum("nl,lhg->nhg", chooser, table)

    def flat(table):
        return table.reshape(table.shape[0], -1)

    zero = jnp.zeros((1,), jnp.int32)
    up_sent, other_sent, own_sent = {}, {}, {}
    wanted_up = {}
    wanted_down = {}
    for name, peers in (("far", far), ("near", near)):
        wanted_up[name] = wanted_of(peers, up_table)
        blocks = pick_blocks(up_weight, flat(wanted_up[name]), zero, runs)
        up_sent.update(zip(peers, blocks))
    for name, peers in (("far", far), ("near", near)):
        wanted_down[name] = wanted_of(peers, core_first)
        other = pick_blocks(down_weight, flat(wanted_down[name][..., own_runs:]), 1 - core[None], own_runs)
        other_sent.update(zip(peers, other))
    for name, peers in (("far", far), ("near", near)):
        own = pick_blocks(down_weight, flat(wanted_down[name][..., :own_runs]), core[None], own_runs)
        own_sent.update(zip(peers, own))
    ranks = [0] + order
    owner = jnp.stack([here ^ k for k in ranks])

    def exchange(sent):
        return [sent[0]] + [swap(sent[k], "dp", dp, k) for k in order]

    up_got = exchange(up_sent)
    other_got = exchange(other_sent)
    own_got = exchange(own_sent)

    peer_acoustic = swap(acoustic, "tensor", 2, 1)
    gains = norm_gain.reshape(2, features)
    gain_own = jnp.where(core == 0, gains[0], gains[1])
    gain_peer = jnp.where(core == 0, gains[1], gains[0])
    wide_own = acoustic.astype(jnp.float32)
    wide_peer = peer_acoustic.astype(jnp.float32)
    square = jnp.sum(wide_own * wide_own, axis=-1, keepdims=True) + jnp.sum(wide_peer * wide_peer, axis=-1, keepdims=True)
    scale = lax.rsqrt(square / (2 * features) + 1e-06)
    normed = jnp.concatenate(
        [
            (wide * scale * gain).astype(jnp.bfloat16).reshape(frames, -1, BLK).transpose(1, 0, 2)
            for wide, gain in ((wide_own, gain_own), (wide_peer, gain_peer))
        ]
    )
    up_own = wanted_up["near"][-1] + jnp.arange(runs, dtype=jnp.int32) * GROUP
    slots = (up_own ^ (core * (feat_blocks // 2))).reshape(-1)
    active = up_project(owner, slots, normed, up_got)
    down_own = wanted_down["near"][-1]
    partial_other = down_project(owner, down_own[:, own_runs:].reshape(-1), active, other_got)
    peer_partial = swap(partial_other, "tensor", 2, 1)
    return down_project(
        owner, down_own[:, :own_runs].reshape(-1), active, own_got, final=(lengths, acoustic, peer_partial)
    )


def exchange_body(acoustic, norm_gain, up_weight, down_weight, up_keep, down_keep, language, lengths):
    frames = acoustic.shape[0]
    nlangs, hidden_blocks, feat_blocks = up_keep.shape
    block_side = BLK
    runs = feat_blocks // GROUP
    whole = lax.all_gather(acoustic, "tensor", axis=1, tiled=True)
    widened = whole.astype(jnp.float32)
    scale = lax.rsqrt(jnp.mean(widened * widened, axis=-1, keepdims=True) + 1e-06)
    normed = (widened * scale * norm_gain).astype(jnp.bfloat16)
    languages = lax.all_gather(language, "dp", axis=0, tiled=True)
    chooser = (languages[:, None] == jnp.arange(nlangs, dtype=jnp.int32)).astype(jnp.int32)
    own_pick = (language[0] == jnp.arange(nlangs, dtype=jnp.int32)).astype(jnp.int32)
    up_table = kept_index(up_keep)
    down_table = kept_index(down_keep)
    up_wanted = jnp.einsum("nl,lhg->nhg", chooser, up_table)
    down_wanted = jnp.einsum("nl,lhg->nhg", chooser, down_table)
    own_up = jnp.einsum("l,lhg->hg", own_pick, up_table)
    own_down = jnp.einsum("l,lhg->hg", own_pick, down_table)
    row_index = jnp.arange(hidden_blocks, dtype=jnp.int32)[None, :, None]
    send_up = up_weight[row_index, up_wanted]
    send_down = down_weight[row_index, down_wanted]
    got_up = lax.all_to_all(send_up, "dp", split_axis=0, concat_axis=3, tiled=True)
    got_down = None
    up_local = got_up[0].reshape(hidden_blocks, runs, block_side, block_side)
    chosen = normed.reshape(frames, feat_blocks, block_side)[:, own_up]
    before = jnp.einsum("thgi,hgij->thj", chosen, up_local, preferred_element_type=jnp.float32)
    active = jax.nn.silu(before).astype(jnp.bfloat16)
    got_down = lax.all_to_all(send_down, "dp", split_axis=0, concat_axis=3, tiled=True)
    down_local = got_down[0].reshape(hidden_blocks, runs, block_side, block_side)
    pieces = []
    for run_at in range(runs):
        contrib = jnp.einsum(
            "thi,hij->thj", active, down_local[:, run_at], preferred_element_type=jnp.float32
        )
        targets = run_at * GROUP + jnp.arange(GROUP, dtype=jnp.int32)
        onehot = (own_down[:, run_at, None] == targets).astype(jnp.float32)
        pieces.append(jnp.einsum("thj,hk->tkj", contrib, onehot, precision=lax.Precision.HIGHEST))
    partial_value = jnp.concatenate(pieces, axis=1).reshape(frames, feat_blocks * block_side)
    feedfwd = lax.psum_scatter(
        partial_value.astype(jnp.bfloat16), "tensor", scatter_dimension=1, tiled=True
    ).astype(jnp.float32)
    valid = (jnp.arange(frames, dtype=jnp.int32) < lengths[0]).astype(jnp.float32)
    return ((acoustic.astype(jnp.float32) + feedfwd) * valid[:, None]).astype(jnp.bfloat16)


def solution(mesh):
    in_specs = (
        P(("parts", "dp"), "tensor"),
        P(),
        P("tensor", None, "dp"),
        P("tensor", None, "dp"),
        P(None, "tensor", None),
        P(None, "tensor", None),
        P(("parts", "dp")),
        P(("parts", "dp")),
    )
    out_specs = P(("parts", "dp"), "tensor")
    dp = mesh.shape["dp"]
    rows = BLK // dp
    whole_tiles = mesh.shape["tensor"] == 2 and dp & (dp - 1) == 0 and rows % 16 == 0
    body = functools.partial(split_body, dp=dp) if whole_tiles else exchange_body
    return jax.shard_map(body, mesh=mesh, in_specs=in_specs, out_specs=out_specs, check_vma=False)
```

```python
import functools

import jax
import jax.numpy as jnp
from jax import lax
from jax.experimental import pallas as pl
from jax.experimental.pallas import tpu as pltpu
from jax.sharding import PartitionSpec as P

BLK = 128
HALF = BLK // 2
GROUP = 8
HSTEP = 4
CHUNKS = 2


def kept_within(keep_mask):
    nlangs, hidden_blocks, feat_blocks = keep_mask.shape
    runs = feat_blocks // GROUP
    picks = jnp.arange(GROUP, dtype=jnp.int32)
    return jnp.sum(keep_mask.reshape(nlangs, hidden_blocks, runs, GROUP) * picks, axis=-1)


def kept_index(keep_mask):
    within = kept_within(keep_mask)
    return within + jnp.arange(within.shape[-1], dtype=jnp.int32) * GROUP


def low_lanes(shape):
    return lax.broadcasted_iota(jnp.int32, shape, len(shape) - 1) < HALF


def half_turn(value):
    return pltpu.roll(value, HALF, value.ndim - 1)


def norm_kernel(side, own_ref, peer_ref, gain_ref, near_ref, far_ref):
    frames, features = own_ref.shape
    slots = features // BLK

    def square(ref):
        total = jnp.zeros((frames, BLK), jnp.float32)
        for d in range(slots):
            wide = ref[:, d * BLK:(d + 1) * BLK].astype(jnp.float32)
            total = total + wide * wide
        return total

    mean = jnp.sum(square(own_ref) + square(peer_ref), axis=-1, keepdims=True) / (2 * features)
    scale = lax.rsqrt(mean + 1e-06)
    low = low_lanes((frames, BLK))
    near_low = low == (side[0] == 0)
    for at, ref in enumerate((own_ref, peer_ref)):
        for d in range(0, slots, 2):
            far = []
            for e in (d, d + 1):
                lanes = slice(e * BLK, (e + 1) * BLK)
                gain = gain_ref[at, :, lanes]
                rounded = (ref[:, lanes].astype(jnp.float32) * scale * gain).astype(jnp.bfloat16).astype(jnp.float32)
                turned = half_turn(rounded)
                near_ref[at * slots + e] = jnp.where(near_low, rounded, turned).astype(jnp.bfloat16)
                far.append(jnp.where(near_low, turned, rounded))
            far_ref[(at * slots + d) // 2] = jnp.where(low, far[0], far[1]).astype(jnp.bfloat16)


def norm_parts(side, own, peer, gains):
    frames, features = own.shape
    slots = 2 * features // BLK
    return pl.pallas_call(
        norm_kernel,
        grid_spec=pltpu.PrefetchScalarGridSpec(
            num_scalar_prefetch=1,
            grid=(1,),
            in_specs=[
                pl.BlockSpec((frames, features), lambda i, *_: (0, 0)),
                pl.BlockSpec((frames, features), lambda i, *_: (0, 0)),
                pl.BlockSpec((2, 1, features), lambda i, *_: (0, 0, 0)),
            ],
            out_specs=[
                pl.BlockSpec((slots, frames, BLK), lambda i, *_: (0, 0, 0)),
                pl.BlockSpec((slots // 2, frames, BLK), lambda i, *_: (0, 0, 0)),
            ],
        ),
        out_shape=[
            jax.ShapeDtypeStruct((slots, frames, BLK), jnp.bfloat16),
            jax.ShapeDtypeStruct((slots // 2, frames, BLK), jnp.bfloat16),
        ],
        name="norm_parts",
    )(side, own, peer, gains)


def pick_kernel(turns, wanted, weight_ref, *refs, rows, runs, base, turning):
    out_refs, spread = refs[:-1], refs[-1]
    step = pl.program_id(0) + base
    for h in range(HSTEP):
        for row in range(rows):
            tile = weight_ref[h, :, row * BLK:(row + 1) * BLK].astype(jnp.float32)
            for g in range(runs):
                spread[h * runs + g, row * GROUP:(row + 1) * GROUP, :] = tile[g * GROUP:(g + 1) * GROUP]
    for k, out_ref in enumerate(out_refs):
        for u in range(2):
            for h in range(HSTEP):
                for g in range(runs):
                    at = wanted[2 * k + u, (step * HSTEP + h) * runs + g]
                    block = spread[h * runs + g, pl.ds(at, rows, stride=GROUP), :]
                    if turning:
                        block = pltpu.roll(block, turns[u], 1)
                    out_ref[u, h, g] = block.astype(jnp.bfloat16)


def pick_blocks(weight, wanted, turns, first, count, turning):
    _, feat_blocks, width = weight.shape
    rows = width // BLK
    runs = feat_blocks // GROUP
    targets = wanted.shape[0] // 2
    base = first // HSTEP
    out_shape = jax.ShapeDtypeStruct((2, count, runs, rows, BLK), jnp.bfloat16)
    out_spec = pl.BlockSpec((2, HSTEP, runs, rows, BLK), lambda i, *_: (0, i, 0, 0, 0))
    return pl.pallas_call(
        functools.partial(pick_kernel, rows=rows, runs=runs, base=base, turning=turning),
        grid_spec=pltpu.PrefetchScalarGridSpec(
            num_scalar_prefetch=2,
            grid=(count // HSTEP,),
            in_specs=[pl.BlockSpec((HSTEP, feat_blocks, width), lambda i, *_: (i + base, 0, 0))],
            out_specs=[out_spec] * targets,
            scratch_shapes=[pltpu.VMEM((HSTEP * runs, rows * GROUP, BLK), jnp.float32)],
        ),
        out_shape=[out_shape] * targets,
        name="pick_up" if turning else "pick_down",
    )(turns, wanted, weight)


def up_kernel(place, slots, own_ref, far_ref, *refs, runs, rows):
    weight_refs, kept_ref, sent_ref, partner, held = refs[:-4], refs[-4], refs[-3], refs[-2], refs[-1]
    step = pl.program_id(0)
    frames = own_ref.shape[1]
    low = low_lanes((frames, BLK))
    side_rows = rows * len(weight_refs)

    @pl.when(step == 0)
    def _():
        for m in range(far_ref.shape[0]):
            pair = far_ref[m].astype(jnp.float32)
            turned = half_turn(pair)
            partner[2 * m] = jnp.where(low, pair, turned).astype(jnp.bfloat16)
            partner[2 * m + 1] = jnp.where(low, turned, pair).astype(jnp.bfloat16)

    for k, ref in enumerate(weight_refs):
        start = pl.multiple_of(place[k] * rows, rows)
        for u in range(2):
            for h in range(HSTEP):
                for g in range(runs):
                    held[u, h, pl.ds(start + g * side_rows, rows), :] = ref[u, h, g]
    for h in range(HSTEP):
        parts = []
        for u, source in enumerate((own_ref, partner)):
            at = [slots[u, (step * HSTEP + h) * runs + g] for g in range(runs)]
            left = jnp.concatenate(
                [jnp.where(low, source[at[g]], source[at[g + 1]]) for g in range(0, runs, 2)], axis=1
            )
            parts.append(jnp.dot(left, held[u, h], preferred_element_type=jnp.float32))
        own, other = parts
        kept_ref[h] = jnp.where(low, other, own)
        sent_ref[h] = jnp.where(low, own, other).astype(jnp.bfloat16)


def up_project(place, slots, own, far, weights):
    _, hidden_blocks, runs, rows, _ = weights[0].shape
    slots_all, frames, _ = own.shape
    out_spec = pl.BlockSpec((HSTEP, frames, BLK), lambda i, *_: (i, 0, 0))
    return pl.pallas_call(
        functools.partial(up_kernel, runs=runs, rows=rows),
        grid_spec=pltpu.PrefetchScalarGridSpec(
            num_scalar_prefetch=2,
            grid=(hidden_blocks // HSTEP,),
            in_specs=[
                pl.BlockSpec((slots_all, frames, BLK), lambda i, *_: (0, 0, 0)),
                pl.BlockSpec((slots_all // 2, frames, BLK), lambda i, *_: (0, 0, 0)),
            ]
            + [pl.BlockSpec((2, HSTEP, runs, rows, BLK), lambda i, *_: (0, i, 0, 0, 0))] * len(weights),
            out_specs=[out_spec, out_spec],
            scratch_shapes=[
                pltpu.VMEM((slots_all, frames, BLK), jnp.bfloat16),
                pltpu.VMEM((2, HSTEP, runs * rows * len(weights), BLK), jnp.bfloat16),
            ],
        ),
        out_shape=[
            jax.ShapeDtypeStruct((hidden_blocks, frames, BLK), jnp.float32),
            jax.ShapeDtypeStruct((hidden_blocks, frames, BLK), jnp.bfloat16),
        ],
        compiler_params=pltpu.CompilerParams(vmem_limit_bytes=48 << 20),
        name="up_project",
    )(place, slots, own, far, *weights)


def down_kernel(which, place, wanted, *refs, utt, parts, runs, rows):
    refs = list(refs)
    step = pl.program_id(0)
    per_part = pl.num_programs(0) // max(parts, 1)
    if parts:
        kept_refs, got_refs, refs = refs[:parts], refs[parts:2 * parts], refs[2 * parts:]
        weight_refs, out_ref, active_ref, held, total = refs[:-4], refs[-4], refs[-3], refs[-2], refs[-1]
        for p in range(parts):
            @pl.when(step // per_part == p)
            def _():
                before = kept_refs[p][...] + got_refs[p][...].astype(jnp.float32)
                active_ref[...] = (before / (1.0 + jnp.exp(-before))).astype(jnp.bfloat16)
    else:
        active_ref, weight_refs, out_ref, held, total = refs[0], refs[1:-3], refs[-3], refs[-2], refs[-1]

    @pl.when(step == 0)
    def _():
        total[...] = jnp.zeros_like(total)
        held[...] = jnp.zeros_like(held)

    top = HALF if utt == 0 else 0
    for k, ref in enumerate(weight_refs):
        start = pl.multiple_of(place[k] * rows, rows)
        for h in range(HSTEP):
            for g in range(runs):
                held[h, pl.ds(start + top, rows), g * BLK:(g + 1) * BLK] = ref[0, h, g]
    all_runs = 2 * runs
    for h in range(HSTEP):
        product = jnp.dot(active_ref[h], held[h], preferred_element_type=jnp.float32)
        for g in range(runs):
            at = g * GROUP + wanted[utt, (step * HSTEP + h) * all_runs + which[0] * runs + g]
            total[at] += product[:, g * BLK:(g + 1) * BLK]

    @pl.when(step == pl.num_programs(0) - 1)
    def _():
        out_ref[...] = total[...].astype(out_ref.dtype)


def down_project(which, place, wanted, sources, weights, utt, out_dtype):
    _, hidden_blocks, all_runs, rows, _ = weights[0].shape
    runs = all_runs // 2
    outs = runs * GROUP
    frames = sources[-1].shape[1]
    parts = len(sources) // 2
    steps = hidden_blocks // HSTEP
    per_part = steps // max(parts, 1)
    active_spec = pl.BlockSpec((HSTEP, frames, BLK), lambda i, *_: (i, 0, 0))
    if parts:
        source_specs = [
            pl.BlockSpec(
                (HSTEP, frames, BLK), lambda i, *_, p=p: (jnp.clip(i - p * per_part, 0, per_part - 1), 0, 0)
            )
            for p in range(parts)
        ] * 2
    else:
        source_specs = [active_spec]
    out_specs = [pl.BlockSpec((outs, frames, BLK), lambda i, *_: (0, 0, 0))]
    out_shape = [jax.ShapeDtypeStruct((outs, frames, BLK), out_dtype)]
    if parts:
        out_specs.append(active_spec)
        out_shape.append(jax.ShapeDtypeStruct((hidden_blocks, frames, BLK), jnp.bfloat16))
    return pl.pallas_call(
        functools.partial(down_kernel, utt=utt, parts=parts, runs=runs, rows=rows),
        grid_spec=pltpu.PrefetchScalarGridSpec(
            num_scalar_prefetch=3,
            grid=(steps,),
            in_specs=source_specs
            + [
                pl.BlockSpec((1, HSTEP, runs, rows, BLK), lambda i, which, *_: (utt, i, which[0], 0, 0))
            ] * len(weights),
            out_specs=out_specs,
            scratch_shapes=[
                pltpu.VMEM((HSTEP, BLK, runs * BLK), jnp.bfloat16),
                pltpu.VMEM((outs, frames, BLK), jnp.float32),
            ],
        ),
        out_shape=out_shape,
        compiler_params=pltpu.CompilerParams(vmem_limit_bytes=48 << 20),
        name=f"down_{utt}",
    )(which, place, wanted, *sources, *weights)


def join_kernel(length, acoustic_ref, mine_ref, core_ref, side_ref, out_ref):
    frames = out_ref.shape[0]
    valid = lax.broadcasted_iota(jnp.int32, (frames, BLK), 0) < length[0]
    for d in range(mine_ref.shape[0]):
        lanes = slice(d * BLK, (d + 1) * BLK)
        feedfwd = mine_ref[d] + core_ref[d].astype(jnp.float32) + side_ref[d].astype(jnp.float32)
        summed = acoustic_ref[:, lanes].astype(jnp.float32) + feedfwd
        out_ref[:, lanes] = jnp.where(valid, summed, 0.0).astype(jnp.bfloat16)


def join(lengths, acoustic, mine, from_core, from_side):
    outs, frames, _ = mine.shape
    per = outs // 4
    block = pl.BlockSpec((per, frames, BLK), lambda i, *_: (i, 0, 0))
    flat = pl.BlockSpec((frames, per * BLK), lambda i, *_: (0, i))
    return pl.pallas_call(
        join_kernel,
        grid_spec=pltpu.PrefetchScalarGridSpec(
            num_scalar_prefetch=1, grid=(4,), in_specs=[flat, block, block, block], out_specs=flat
        ),
        out_shape=jax.ShapeDtypeStruct(acoustic.shape, jnp.bfloat16),
        name="join",
    )(lengths, acoustic, mine, from_core, from_side)


def swap(value, axis, size, step):
    return lax.ppermute(value, axis, [(i, i ^ step) for i in range(size)])


def split_body(acoustic, norm_gain, up_weight, down_weight, up_keep, down_keep, language, lengths, *, dp):
    frames, features = acoustic.shape
    nlangs, hidden_blocks, feat_blocks = up_keep.shape
    runs = feat_blocks // GROUP
    across = dp // 2
    members = list(range(across))
    here = lax.axis_index("dp").astype(jnp.int32)
    core = lax.axis_index("tensor").astype(jnp.int32)
    side = (here // across)[None]

    heard = {0: language}
    for k in [across] + members[1:] + [across + k for k in members[1:]]:
        heard[k] = swap(language, "dp", dp, k)
    langs = jnp.concatenate([heard[k ^ far] for k in members for far in (0, across)])
    chooser = (langs[:, None] == jnp.arange(nlangs, dtype=jnp.int32)).astype(jnp.int32)
    wanted_up = jnp.einsum("nl,lhg->nhg", chooser, kept_within(up_keep))
    wanted_down = jnp.einsum("nl,lhg->nhg", chooser, kept_within(down_keep))
    up_own = wanted_up[:2] + jnp.arange(runs, dtype=jnp.int32) * GROUP
    slots = (up_own ^ (core * (feat_blocks // 2))).reshape(2, -1)
    wanted_up = wanted_up.reshape(2 * across, -1)
    wanted_down = wanted_down.reshape(2 * across, -1)
    place = jnp.stack([(here ^ k) % across for k in members])
    turns = jnp.stack([HALF * (1 - side[0]), HALF * side[0]])

    peer = swap(acoustic, "tensor", 2, 1)
    gains = norm_gain.reshape(2, 1, features)
    gains = jnp.where(core == 0, gains, gains[::-1])
    near, far = norm_parts(side, acoustic, peer, gains)
    far = swap(far, "dp", dp, across)

    def within_side(blocks):
        return [blocks[0]] + [swap(blocks[k], "dp", dp, k) for k in members[1:]]

    count = hidden_blocks // CHUNKS
    kept, crossed, last = [], [], None
    for c in range(CHUNKS):
        blocks = pick_blocks(up_weight, wanted_up, turns, c * count, count, True)
        got = within_side(blocks)
        last = got
        mine, sent = up_project(place, slots[:, c * count * runs:(c + 1) * count * runs], near, far, got)
        kept.append(mine)
        crossed.append(swap(sent, "dp", dp, across))
    blocks = pick_blocks(down_weight, wanted_down, turns, 0, hidden_blocks, False)
    blocks, _ = lax.optimization_barrier((blocks, last))
    got = within_side(blocks)
    other_core = (1 - core)[None]
    this_core = core[None]
    rows_down = wanted_down[:2]
    for_peer, active = down_project(other_core, place, rows_down, kept + crossed, got, 1, jnp.bfloat16)
    from_peer = swap(for_peer, "tensor", 2, 1)
    (partner_mine,) = down_project(this_core, place, rows_down, [active], got, 1, jnp.float32)
    for_side = (partner_mine + from_peer.astype(jnp.float32)).astype(jnp.bfloat16)
    from_side = swap(for_side, "dp", dp, across)
    (own_peer,) = down_project(other_core, place, rows_down, [active], got, 0, jnp.bfloat16)
    from_core = swap(own_peer, "tensor", 2, 1)
    (own_mine,) = down_project(this_core, place, rows_down, [active], got, 0, jnp.float32)
    return join(lengths, acoustic, own_mine, from_core, from_side)


def exchange_body(acoustic, norm_gain, up_weight, down_weight, up_keep, down_keep, language, lengths):
    frames = acoustic.shape[0]
    nlangs, hidden_blocks, feat_blocks = up_keep.shape
    block_side = BLK
    runs = feat_blocks // GROUP
    whole = lax.all_gather(acoustic, "tensor", axis=1, tiled=True)
    widened = whole.astype(jnp.float32)
    scale = lax.rsqrt(jnp.mean(widened * widened, axis=-1, keepdims=True) + 1e-06)
    normed = (widened * scale * norm_gain).astype(jnp.bfloat16)
    languages = lax.all_gather(language, "dp", axis=0, tiled=True)
    chooser = (languages[:, None] == jnp.arange(nlangs, dtype=jnp.int32)).astype(jnp.int32)
    own_pick = (language[0] == jnp.arange(nlangs, dtype=jnp.int32)).astype(jnp.int32)
    up_table = kept_index(up_keep)
    down_table = kept_index(down_keep)
    up_wanted = jnp.einsum("nl,lhg->nhg", chooser, up_table)
    down_wanted = jnp.einsum("nl,lhg->nhg", chooser, down_table)
    own_up = jnp.einsum("l,lhg->hg", own_pick, up_table)
    own_down = jnp.einsum("l,lhg->hg", own_pick, down_table)
    row_index = jnp.arange(hidden_blocks, dtype=jnp.int32)[None, :, None]
    send_up = up_weight[row_index, up_wanted]
    send_down = down_weight[row_index, down_wanted]
    got_up = lax.all_to_all(send_up, "dp", split_axis=0, concat_axis=3, tiled=True)
    got_down = None
    up_local = got_up[0].reshape(hidden_blocks, runs, block_side, block_side)
    chosen = normed.reshape(frames, feat_blocks, block_side)[:, own_up]
    before = jnp.einsum("thgi,hgij->thj", chosen, up_local, preferred_element_type=jnp.float32)
    active = jax.nn.silu(before).astype(jnp.bfloat16)
    got_down = lax.all_to_all(send_down, "dp", split_axis=0, concat_axis=3, tiled=True)
    down_local = got_down[0].reshape(hidden_blocks, runs, block_side, block_side)
    pieces = []
    for run_at in range(runs):
        contrib = jnp.einsum(
            "thi,hij->thj", active, down_local[:, run_at], preferred_element_type=jnp.float32
        )
        targets = run_at * GROUP + jnp.arange(GROUP, dtype=jnp.int32)
        onehot = (own_down[:, run_at, None] == targets).astype(jnp.float32)
        pieces.append(jnp.einsum("thj,hk->tkj", contrib, onehot, precision=lax.Precision.HIGHEST))
    partial_value = jnp.concatenate(pieces, axis=1).reshape(frames, feat_blocks * block_side)
    feedfwd = lax.psum_scatter(
        partial_value.astype(jnp.bfloat16), "tensor", scatter_dimension=1, tiled=True
    ).astype(jnp.float32)
    valid = (jnp.arange(frames, dtype=jnp.int32) < lengths[0]).astype(jnp.float32)
    return ((acoustic.astype(jnp.float32) + feedfwd) * valid[:, None]).astype(jnp.bfloat16)


def solution(mesh):
    in_specs = (
        P(("parts", "dp"), "tensor"),
        P(),
        P("tensor", None, "dp"),
        P("tensor", None, "dp"),
        P(None, "tensor", None),
        P(None, "tensor", None),
        P(("parts", "dp")),
        P(("parts", "dp")),
    )
    out_specs = P(("parts", "dp"), "tensor")
    dp = mesh.shape["dp"]
    rows = BLK // dp
    whole_tiles = mesh.shape["tensor"] == 2 and dp & (dp - 1) == 0 and dp > 1 and rows % 16 == 0
    body = functools.partial(split_body, dp=dp) if whole_tiles else exchange_body
    return jax.shard_map(body, mesh=mesh, in_specs=in_specs, out_specs=out_specs, check_vma=False)
```

```python
import functools

import jax
import jax.numpy as jnp
from jax import lax
from jax.experimental import pallas as pl
from jax.experimental.pallas import tpu as pltpu
from jax.sharding import PartitionSpec as P

BLK = 128
HALF = BLK // 2
GROUP = 8
HSTEP = 8
CHUNKS = 2


def kept_within(keep_mask):
    nlangs, hidden_blocks, feat_blocks = keep_mask.shape
    runs = feat_blocks // GROUP
    picks = jnp.arange(GROUP, dtype=jnp.int32)
    return jnp.sum(keep_mask.reshape(nlangs, hidden_blocks, runs, GROUP) * picks, axis=-1)


def kept_index(keep_mask):
    within = kept_within(keep_mask)
    return within + jnp.arange(within.shape[-1], dtype=jnp.int32) * GROUP


def low_lanes(shape):
    return lax.broadcasted_iota(jnp.int32, shape, len(shape) - 1) < HALF


def half_turn(value):
    return pltpu.roll(value, HALF, value.ndim - 1)


def norm_kernel(side, own_ref, peer_ref, gain_ref, near_ref, far_ref):
    frames, features = own_ref.shape
    slots = features // BLK

    def square(ref):
        total = jnp.zeros((frames, BLK), jnp.float32)
        for d in range(slots):
            wide = ref[:, d * BLK:(d + 1) * BLK].astype(jnp.float32)
            total = total + wide * wide
        return total

    mean = jnp.sum(square(own_ref) + square(peer_ref), axis=-1, keepdims=True) / (2 * features)
    scale = lax.rsqrt(mean + 1e-06)
    low = low_lanes((frames, BLK))
    near_low = low == (side[0] == 0)
    for at, ref in enumerate((own_ref, peer_ref)):
        for d in range(0, slots, 2):
            far = []
            for e in (d, d + 1):
                lanes = slice(e * BLK, (e + 1) * BLK)
                gain = gain_ref[at, :, lanes]
                rounded = (ref[:, lanes].astype(jnp.float32) * scale * gain).astype(jnp.bfloat16).astype(jnp.float32)
                turned = half_turn(rounded)
                near_ref[at * slots + e] = jnp.where(near_low, rounded, turned).astype(jnp.bfloat16)
                far.append(jnp.where(near_low, turned, rounded))
            far_ref[(at * slots + d) // 2] = jnp.where(low, far[0], far[1]).astype(jnp.bfloat16)


def norm_parts(side, own, peer, gains):
    frames, features = own.shape
    slots = 2 * features // BLK
    return pl.pallas_call(
        norm_kernel,
        grid_spec=pltpu.PrefetchScalarGridSpec(
            num_scalar_prefetch=1,
            grid=(1,),
            in_specs=[
                pl.BlockSpec((frames, features), lambda i, *_: (0, 0)),
                pl.BlockSpec((frames, features), lambda i, *_: (0, 0)),
                pl.BlockSpec((2, 1, features), lambda i, *_: (0, 0, 0)),
            ],
            out_specs=[
                pl.BlockSpec((slots, frames, BLK), lambda i, *_: (0, 0, 0)),
                pl.BlockSpec((slots // 2, frames, BLK), lambda i, *_: (0, 0, 0)),
            ],
        ),
        out_shape=[
            jax.ShapeDtypeStruct((slots, frames, BLK), jnp.bfloat16),
            jax.ShapeDtypeStruct((slots // 2, frames, BLK), jnp.bfloat16),
        ],
        name="norm_parts",
    )(side, own, peer, gains)


def pick_kernel(wanted, weight_ref, *refs, rows, runs, base, turning):
    out_refs, spread = refs[:-1], refs[-1]
    step = pl.program_id(0) + base
    for h in range(HSTEP):
        for row in range(rows):
            tile = weight_ref[h, :, row * BLK:(row + 1) * BLK].astype(jnp.float32)
            for g in range(runs):
                spread[h * runs + g, row * GROUP:(row + 1) * GROUP, :] = tile[g * GROUP:(g + 1) * GROUP]
    for k, out_ref in enumerate(out_refs):
        for u in range(2):
            for h in range(HSTEP):
                for g in range(runs):
                    at = wanted[2 * k + u, (step * HSTEP + h) * runs + g]
                    block = spread[h * runs + g, pl.ds(at, rows, stride=GROUP), :]
                    if turning and h % 2:
                        block = half_turn(block)
                    out_ref[u, h, g] = block.astype(jnp.bfloat16)


def pick_blocks(weight, wanted, first, count, turning):
    _, feat_blocks, width = weight.shape
    rows = width // BLK
    runs = feat_blocks // GROUP
    targets = wanted.shape[0] // 2
    base = first // HSTEP
    out_shape = jax.ShapeDtypeStruct((2, count, runs, rows, BLK), jnp.bfloat16)
    out_spec = pl.BlockSpec((2, HSTEP, runs, rows, BLK), lambda i, *_: (0, i, 0, 0, 0))
    return pl.pallas_call(
        functools.partial(pick_kernel, rows=rows, runs=runs, base=base, turning=turning),
        grid_spec=pltpu.PrefetchScalarGridSpec(
            num_scalar_prefetch=1,
            grid=(count // HSTEP,),
            in_specs=[pl.BlockSpec((HSTEP, feat_blocks, width), lambda i, *_: (i + base, 0, 0))],
            out_specs=[out_spec] * targets,
            scratch_shapes=[pltpu.VMEM((HSTEP * runs, rows * GROUP, BLK), jnp.float32)],
        ),
        out_shape=[out_shape] * targets,
        name="pick_up" if turning else "pick_down",
    )(wanted, weight)


def up_kernel(side, place, slots, own_ref, far_ref, *refs, runs, rows):
    weight_refs, refs = refs[:-6], refs[-6:]
    kept_refs, sent_refs, partner, held = refs[:2], refs[2:4], refs[4], refs[5]
    step = pl.program_id(0)
    frames = own_ref.shape[1]
    low = low_lanes((frames, BLK))
    even = low == (side[0] == 0)
    side_rows = rows * len(weight_refs)

    @pl.when(step == 0)
    def _():
        for m in range(far_ref.shape[0]):
            pair = far_ref[m].astype(jnp.float32)
            turned = half_turn(pair)
            partner[2 * m] = jnp.where(low, pair, turned).astype(jnp.bfloat16)
            partner[2 * m + 1] = jnp.where(low, turned, pair).astype(jnp.bfloat16)

    for k, ref in enumerate(weight_refs):
        start = pl.multiple_of(place[k] * rows, rows)
        for u in range(2):
            for h in range(HSTEP):
                for g in range(runs):
                    held[u, h, pl.ds(start + g * side_rows, rows), :] = ref[u, h, g]
    for m in range(HSTEP // 2):
        for u, source in enumerate((own_ref, partner)):
            pair = []
            for h in (2 * m, 2 * m + 1):
                at = [slots[u, (step * HSTEP + h) * runs + g] for g in range(runs)]
                left = jnp.concatenate(
                    [jnp.where(low, source[at[g]], source[at[g + 1]]) for g in range(0, runs, 2)], axis=1
                )
                pair.append(jnp.dot(left, held[u, h], preferred_element_type=jnp.float32))
            kept_refs[u][m] = jnp.where(even, pair[0], pair[1])
            sent_refs[u][m] = jnp.where(even, pair[1], pair[0]).astype(jnp.bfloat16)


def up_project(side, place, slots, own, far, weights):
    _, hidden_blocks, runs, rows, _ = weights[0].shape
    slots_all, frames, _ = own.shape
    out_spec = pl.BlockSpec((HSTEP // 2, frames, BLK), lambda i, *_: (i, 0, 0))
    return pl.pallas_call(
        functools.partial(up_kernel, runs=runs, rows=rows),
        grid_spec=pltpu.PrefetchScalarGridSpec(
            num_scalar_prefetch=3,
            grid=(hidden_blocks // HSTEP,),
            in_specs=[
                pl.BlockSpec((slots_all, frames, BLK), lambda i, *_: (0, 0, 0)),
                pl.BlockSpec((slots_all // 2, frames, BLK), lambda i, *_: (0, 0, 0)),
            ]
            + [pl.BlockSpec((2, HSTEP, runs, rows, BLK), lambda i, *_: (0, i, 0, 0, 0))] * len(weights),
            out_specs=[out_spec] * 4,
            scratch_shapes=[
                pltpu.VMEM((slots_all, frames, BLK), jnp.bfloat16),
                pltpu.VMEM((2, HSTEP, runs * rows * len(weights), BLK), jnp.bfloat16),
            ],
        ),
        out_shape=[jax.ShapeDtypeStruct((hidden_blocks // 2, frames, BLK), jnp.float32)] * 2
        + [jax.ShapeDtypeStruct((hidden_blocks // 2, frames, BLK), jnp.bfloat16)] * 2,
        compiler_params=pltpu.CompilerParams(vmem_limit_bytes=48 << 20),
        name="up_project",
    )(side, place, slots, own, far, *weights)


def down_kernel(side, which, place, wanted, *refs, utt, parts, runs, rows):
    refs = list(refs)
    step = pl.program_id(0)
    if parts:
        kept_refs, got_refs, refs = refs[:parts], refs[parts:2 * parts], refs[2 * parts:]
        weight_refs, out_ref, active_ref, held, total = refs[:-4], refs[-4], refs[-3], refs[-2], refs[-1]
        per_part = pl.num_programs(0) // parts
        for p in range(parts):
            @pl.when(step // per_part == p)
            def _():
                before = kept_refs[p][...] + got_refs[p][...].astype(jnp.float32)
                active_ref[...] = (before / (1.0 + jnp.exp(-before))).astype(jnp.bfloat16)
    else:
        active_ref, weight_refs, out_ref, held, total = refs[0], refs[1:-3], refs[-3], refs[-2], refs[-1]

    @pl.when(step == 0)
    def _():
        total[...] = jnp.zeros_like(total)
        held[...] = jnp.zeros_like(held)

    for k, ref in enumerate(weight_refs):
        for h in range(HSTEP):
            top = HALF * (side[0] ^ (h % 2))
            start = pl.multiple_of(place[k] * rows + top, rows)
            for g in range(runs):
                at = (h % 2) * runs + g
                held[h // 2, pl.ds(start, rows), at * BLK:(at + 1) * BLK] = ref[0, h, g]
    all_runs = 2 * runs
    for m in range(HSTEP // 2):
        product = jnp.dot(active_ref[m], held[m], preferred_element_type=jnp.float32)
        for odd in range(2):
            for g in range(runs):
                h = step * HSTEP + 2 * m + odd
                at = g * GROUP + wanted[utt, h * all_runs + which[0] * runs + g]
                lane = (odd * runs + g) * BLK
                total[at] += product[:, lane:lane + BLK]

    @pl.when(step == pl.num_programs(0) - 1)
    def _():
        out_ref[...] = total[...].astype(out_ref.dtype)


def down_project(side, which, place, wanted, sources, weights, utt, out_dtype):
    _, hidden_blocks, all_runs, rows, _ = weights[0].shape
    runs = all_runs // 2
    outs = runs * GROUP
    frames = sources[-1].shape[1]
    parts = len(sources) // 2
    steps = hidden_blocks // HSTEP
    per_part = steps // max(parts, 1)
    half_step = HSTEP // 2
    active_spec = pl.BlockSpec((half_step, frames, BLK), lambda i, *_: (i, 0, 0))
    if parts:
        source_specs = [
            pl.BlockSpec(
                (half_step, frames, BLK), lambda i, *_, p=p: (jnp.clip(i - p * per_part, 0, per_part - 1), 0, 0)
            )
            for p in range(parts)
        ] * 2
    else:
        source_specs = [active_spec]
    out_specs = [pl.BlockSpec((outs, frames, BLK), lambda i, *_: (0, 0, 0))]
    out_shape = [jax.ShapeDtypeStruct((outs, frames, BLK), out_dtype)]
    if parts:
        out_specs.append(active_spec)
        out_shape.append(jax.ShapeDtypeStruct((hidden_blocks // 2, frames, BLK), jnp.bfloat16))
    return pl.pallas_call(
        functools.partial(down_kernel, utt=utt, parts=parts, runs=runs, rows=rows),
        grid_spec=pltpu.PrefetchScalarGridSpec(
            num_scalar_prefetch=4,
            grid=(steps,),
            in_specs=source_specs
            + [
                pl.BlockSpec((1, HSTEP, runs, rows, BLK), lambda i, side, which, *_: (utt, i, which[0], 0, 0))
            ] * len(weights),
            out_specs=out_specs,
            scratch_shapes=[
                pltpu.VMEM((half_step, BLK, 2 * runs * BLK), jnp.bfloat16),
                pltpu.VMEM((outs, frames, BLK), jnp.float32),
            ],
        ),
        out_shape=out_shape,
        compiler_params=pltpu.CompilerParams(vmem_limit_bytes=48 << 20),
        name=f"down_{utt}",
    )(side, which, place, wanted, *sources, *weights)


def join_kernel(length, acoustic_ref, mine_ref, core_ref, side_ref, out_ref):
    frames = out_ref.shape[0]
    valid = lax.broadcasted_iota(jnp.int32, (frames, BLK), 0) < length[0]
    for d in range(mine_ref.shape[0]):
        lanes = slice(d * BLK, (d + 1) * BLK)
        feedfwd = mine_ref[d] + core_ref[d].astype(jnp.float32) + side_ref[d].astype(jnp.float32)
        summed = acoustic_ref[:, lanes].astype(jnp.float32) + feedfwd
        out_ref[:, lanes] = jnp.where(valid, summed, 0.0).astype(jnp.bfloat16)


def join(lengths, acoustic, mine, from_core, from_side):
    outs, frames, _ = mine.shape
    per = outs // 4
    block = pl.BlockSpec((per, frames, BLK), lambda i, *_: (i, 0, 0))
    flat = pl.BlockSpec((frames, per * BLK), lambda i, *_: (0, i))
    return pl.pallas_call(
        join_kernel,
        grid_spec=pltpu.PrefetchScalarGridSpec(
            num_scalar_prefetch=1, grid=(4,), in_specs=[flat, block, block, block], out_specs=flat
        ),
        out_shape=jax.ShapeDtypeStruct(acoustic.shape, jnp.bfloat16),
        name="join",
    )(lengths, acoustic, mine, from_core, from_side)


def swap(value, axis, size, step):
    return lax.ppermute(value, axis, [(i, i ^ step) for i in range(size)])


def split_body(acoustic, norm_gain, up_weight, down_weight, up_keep, down_keep, language, lengths, *, dp):
    frames, features = acoustic.shape
    nlangs, hidden_blocks, feat_blocks = up_keep.shape
    runs = feat_blocks // GROUP
    across = dp // 2
    members = list(range(across))
    here = lax.axis_index("dp").astype(jnp.int32)
    core = lax.axis_index("tensor").astype(jnp.int32)
    side = (here // across)[None]

    langs = language
    step = across
    while step != 0:
        langs = jnp.concatenate([langs, swap(langs, "dp", dp, step)])
        step = 1 if step == across else 2 * step
        step = 0 if step == across else step
    chooser = (langs[:, None] == jnp.arange(nlangs, dtype=jnp.int32)).astype(jnp.int32)
    wanted_up = jnp.einsum("nl,lhg->nhg", chooser, kept_within(up_keep))
    wanted_down = jnp.einsum("nl,lhg->nhg", chooser, kept_within(down_keep))
    up_own = wanted_up[:2] + jnp.arange(runs, dtype=jnp.int32) * GROUP
    slots = (up_own ^ (core * (feat_blocks // 2))).reshape(2, -1)
    wanted_up = wanted_up.reshape(2 * across, -1)
    wanted_down = wanted_down.reshape(2 * across, -1)
    place = jnp.stack([(here ^ k) % across for k in members])
    peer = swap(acoustic, "tensor", 2, 1)
    gains = norm_gain.reshape(2, 1, features)
    gains = jnp.where(core == 0, gains, gains[::-1])
    near, own_far = norm_parts(side, acoustic, peer, gains)
    far = swap(own_far, "dp", dp, across)
    wanted_up, _ = lax.optimization_barrier((wanted_up, own_far))

    def within_side(blocks):
        return [blocks[0]] + [swap(blocks[k], "dp", dp, k) for k in members[1:]]

    count = hidden_blocks // CHUNKS
    kept, crossed, last = ([], []), ([], []), None
    for c in range(CHUNKS):
        blocks = pick_blocks(up_weight, wanted_up, c * count, count, True)
        got = within_side(blocks)
        last = got
        span = slice(c * count * runs, (c + 1) * count * runs)
        kept_own, kept_far, sent_own, sent_far = up_project(side, place, slots[:, span], near, far, got)
        got_far = swap(sent_own, "dp", dp, across)
        sent_far, _ = lax.optimization_barrier((sent_far, got_far))
        got_own = swap(sent_far, "dp", dp, across)
        for u, (mine, theirs) in enumerate(((kept_own, got_own), (kept_far, got_far))):
            kept[u].append(mine)
            crossed[u].append(theirs)
    blocks = pick_blocks(down_weight, wanted_down, 0, hidden_blocks, False)
    blocks, _ = lax.optimization_barrier((blocks, last))
    got = within_side(blocks)
    rows_down = wanted_down[:2]

    def down(which, sources, utt, dtype):
        return down_project(side, which, place, rows_down, sources, got, utt, dtype)

    other_core = (1 - core)[None]
    this_core = core[None]
    for_peer, active_far = down(other_core, kept[1] + crossed[1], 1, jnp.bfloat16)
    from_peer = swap(for_peer, "tensor", 2, 1)
    (far_mine,) = down(this_core, [active_far], 1, jnp.float32)
    for_side = (far_mine + from_peer.astype(jnp.float32)).astype(jnp.bfloat16)
    from_side = swap(for_side, "dp", dp, across)
    own_peer, active_own = down(other_core, kept[0] + crossed[0], 0, jnp.bfloat16)
    from_core = swap(own_peer, "tensor", 2, 1)
    (own_mine,) = down(this_core, [active_own], 0, jnp.float32)
    return join(lengths, acoustic, own_mine, from_core, from_side)


def exchange_body(acoustic, norm_gain, up_weight, down_weight, up_keep, down_keep, language, lengths):
    frames = acoustic.shape[0]
    nlangs, hidden_blocks, feat_blocks = up_keep.shape
    block_side = BLK
    runs = feat_blocks // GROUP
    whole = lax.all_gather(acoustic, "tensor", axis=1, tiled=True)
    widened = whole.astype(jnp.float32)
    scale = lax.rsqrt(jnp.mean(widened * widened, axis=-1, keepdims=True) + 1e-06)
    normed = (widened * scale * norm_gain).astype(jnp.bfloat16)
    languages = lax.all_gather(language, "dp", axis=0, tiled=True)
    chooser = (languages[:, None] == jnp.arange(nlangs, dtype=jnp.int32)).astype(jnp.int32)
    own_pick = (language[0] == jnp.arange(nlangs, dtype=jnp.int32)).astype(jnp.int32)
    up_table = kept_index(up_keep)
    down_table = kept_index(down_keep)
    up_wanted = jnp.einsum("nl,lhg->nhg", chooser, up_table)
    down_wanted = jnp.einsum("nl,lhg->nhg", chooser, down_table)
    own_up = jnp.einsum("l,lhg->hg", own_pick, up_table)
    own_down = jnp.einsum("l,lhg->hg", own_pick, down_table)
    row_index = jnp.arange(hidden_blocks, dtype=jnp.int32)[None, :, None]
    send_up = up_weight[row_index, up_wanted]
    send_down = down_weight[row_index, down_wanted]
    got_up = lax.all_to_all(send_up, "dp", split_axis=0, concat_axis=3, tiled=True)
    got_down = None
    up_local = got_up[0].reshape(hidden_blocks, runs, block_side, block_side)
    chosen = normed.reshape(frames, feat_blocks, block_side)[:, own_up]
    before = jnp.einsum("thgi,hgij->thj", chosen, up_local, preferred_element_type=jnp.float32)
    active = jax.nn.silu(before).astype(jnp.bfloat16)
    got_down = lax.all_to_all(send_down, "dp", split_axis=0, concat_axis=3, tiled=True)
    down_local = got_down[0].reshape(hidden_blocks, runs, block_side, block_side)
    pieces = []
    for run_at in range(runs):
        contrib = jnp.einsum(
            "thi,hij->thj", active, down_local[:, run_at], preferred_element_type=jnp.float32
        )
        targets = run_at * GROUP + jnp.arange(GROUP, dtype=jnp.int32)
        onehot = (own_down[:, run_at, None] == targets).astype(jnp.float32)
        pieces.append(jnp.einsum("thj,hk->tkj", contrib, onehot, precision=lax.Precision.HIGHEST))
    partial_value = jnp.concatenate(pieces, axis=1).reshape(frames, feat_blocks * block_side)
    feedfwd = lax.psum_scatter(
        partial_value.astype(jnp.bfloat16), "tensor", scatter_dimension=1, tiled=True
    ).astype(jnp.float32)
    valid = (jnp.arange(frames, dtype=jnp.int32) < lengths[0]).astype(jnp.float32)
    return ((acoustic.astype(jnp.float32) + feedfwd) * valid[:, None]).astype(jnp.bfloat16)


def solution(mesh):
    in_specs = (
        P(("parts", "dp"), "tensor"),
        P(),
        P("tensor", None, "dp"),
        P("tensor", None, "dp"),
        P(None, "tensor", None),
        P(None, "tensor", None),
        P(("parts", "dp")),
        P(("parts", "dp")),
    )
    out_specs = P(("parts", "dp"), "tensor")
    dp = mesh.shape["dp"]
    rows = BLK // dp
    whole_tiles = mesh.shape["tensor"] == 2 and dp & (dp - 1) == 0 and dp > 1 and rows % 16 == 0
    body = functools.partial(split_body, dp=dp) if whole_tiles else exchange_body
    return jax.shard_map(body, mesh=mesh, in_specs=in_specs, out_specs=out_specs, check_vma=False)
```

```python
import functools

import jax
import jax.numpy as jnp
from jax import lax
from jax.experimental import pallas as pl
from jax.experimental.pallas import tpu as pltpu
from jax.sharding import PartitionSpec as P

BLK = 128
HALF = BLK // 2
GROUP = 8
HSTEP = 8
CHUNKS = 2


def kept_within(keep_mask):
    nlangs, hidden_blocks, feat_blocks = keep_mask.shape
    runs = feat_blocks // GROUP
    picks = jnp.arange(GROUP, dtype=jnp.int32)
    return jnp.sum(keep_mask.reshape(nlangs, hidden_blocks, runs, GROUP) * picks, axis=-1)


def kept_index(keep_mask):
    within = kept_within(keep_mask)
    return within + jnp.arange(within.shape[-1], dtype=jnp.int32) * GROUP


def low_lanes(shape):
    return lax.broadcasted_iota(jnp.int32, shape, len(shape) - 1) < HALF


def half_turn(value):
    return pltpu.roll(value, HALF, value.ndim - 1)


def norm_kernel(side, own_ref, peer_ref, gain_ref, near_ref, far_ref):
    frames, features = own_ref.shape
    slots = features // BLK

    def square(ref):
        total = jnp.zeros((frames, BLK), jnp.float32)
        for d in range(slots):
            wide = ref[:, d * BLK:(d + 1) * BLK].astype(jnp.float32)
            total = total + wide * wide
        return total

    mean = jnp.sum(square(own_ref) + square(peer_ref), axis=-1, keepdims=True) / (2 * features)
    scale = lax.rsqrt(mean + 1e-06)
    low = low_lanes((frames, BLK))
    near_low = low == (side[0] == 0)
    for at, ref in enumerate((own_ref, peer_ref)):
        for d in range(0, slots, 2):
            far = []
            for e in (d, d + 1):
                lanes = slice(e * BLK, (e + 1) * BLK)
                gain = gain_ref[at, :, lanes]
                rounded = (ref[:, lanes].astype(jnp.float32) * scale * gain).astype(jnp.bfloat16).astype(jnp.float32)
                turned = half_turn(rounded)
                near_ref[at * slots + e] = jnp.where(near_low, rounded, turned).astype(jnp.bfloat16)
                far.append(jnp.where(near_low, turned, rounded))
            if at == 0:
                far_ref[d // 2] = jnp.where(low, far[0], far[1]).astype(jnp.bfloat16)


def norm_parts(side, own, peer, gains):
    frames, features = own.shape
    slots = 2 * features // BLK
    return pl.pallas_call(
        norm_kernel,
        grid_spec=pltpu.PrefetchScalarGridSpec(
            num_scalar_prefetch=1,
            grid=(1,),
            in_specs=[
                pl.BlockSpec((frames, features), lambda i, *_: (0, 0)),
                pl.BlockSpec((frames, features), lambda i, *_: (0, 0)),
                pl.BlockSpec((2, 1, features), lambda i, *_: (0, 0, 0)),
            ],
            out_specs=[
                pl.BlockSpec((slots, frames, BLK), lambda i, *_: (0, 0, 0)),
                pl.BlockSpec((slots // 4, frames, BLK), lambda i, *_: (0, 0, 0)),
            ],
        ),
        out_shape=[
            pltpu.HBM((slots, frames, BLK), jnp.bfloat16),
            pltpu.HBM((slots // 4, frames, BLK), jnp.bfloat16),
        ],
        name="norm_parts",
    )(side, own, peer, gains)


def pick_kernel(place, wanted, weight_ref, *refs, rows, runs, base, turning, after):
    out_refs, spread = refs[after:-1], refs[-1]
    step = pl.program_id(0) + base
    for h in range(HSTEP):
        for row in range(rows):
            tile = weight_ref[h, :, row * BLK:(row + 1) * BLK].astype(jnp.float32)
            for g in range(runs):
                spread[h * runs + g, row * GROUP:(row + 1) * GROUP, :] = tile[g * GROUP:(g + 1) * GROUP]
    for member in range(wanted.shape[0] // 2):
        pair = 2 * (place[0] ^ member)
        for u in range(2):
            for h in range(HSTEP):
                for g in range(runs):
                    at = wanted[pair + u, (step * HSTEP + h) * runs + g]
                    block = spread[h * runs + g, pl.ds(at, rows, stride=GROUP), :]
                    if turning and h % 2:
                        block = half_turn(block)
                    block = block.astype(jnp.bfloat16)
                    if turning:
                        out_refs[0][member, u, h, g] = block
                    else:
                        out_refs[u][member, h, g] = block


def pick_blocks(weight, place, wanted, first, count, turning, after=()):
    _, feat_blocks, width = weight.shape
    rows = width // BLK
    runs = feat_blocks // GROUP
    base = first // HSTEP
    members = wanted.shape[0] // 2
    if turning:
        outs = 1
        shape = (members, 2, count, runs, rows, BLK)
        out_spec = pl.BlockSpec((members, 2, HSTEP, runs, rows, BLK), lambda i, *_: (0, 0, i, 0, 0, 0))
    else:
        outs = 2
        shape = (members, count, runs, rows, BLK)
        out_spec = pl.BlockSpec((members, HSTEP, runs, rows, BLK), lambda i, *_: (0, i, 0, 0, 0))
    return pl.pallas_call(
        functools.partial(pick_kernel, rows=rows, runs=runs, base=base, turning=turning, after=len(after)),
        grid_spec=pltpu.PrefetchScalarGridSpec(
            num_scalar_prefetch=2,
            grid=(count // HSTEP,),
            in_specs=[pl.BlockSpec((HSTEP, feat_blocks, width), lambda i, *_: (i + base, 0, 0))]
            + [corner(value) for value in after],
            out_specs=[out_spec] * outs,
            scratch_shapes=[pltpu.VMEM((HSTEP * runs, rows * GROUP, BLK), jnp.float32)],
        ),
        out_shape=[pltpu.HBM(shape, jnp.bfloat16)] * outs,
        compiler_params=pltpu.CompilerParams(vmem_limit_bytes=48 << 20),
        name="pick_up" if turning else "pick_down",
    )(place, wanted, *in_hbm([weight]), *after)


def corner(value):
    zeros = (0,) * value.ndim
    return pl.BlockSpec((1,) * (value.ndim - 2) + (16, BLK), lambda i, *_: zeros)


def gate_kernel(*refs):
    del refs


def gate(values, after):
    anywhere = pl.BlockSpec(memory_space=pl.ANY)
    return pl.pallas_call(
        gate_kernel,
        grid=(1,),
        in_specs=[anywhere] * len(values) + [corner(value) for value in after],
        out_specs=[anywhere] * len(values),
        out_shape=[pltpu.HBM(value.shape, value.dtype) for value in values],
        input_output_aliases={i: i for i in range(len(values))},
        name="gate",
    )(*in_hbm(values), *after)


def up_kernel(side, slots, own_ref, far_a_ref, far_b_ref, weight_ref, *refs, runs, rows):
    kept_refs, sent_refs, partner, held = refs[:2], refs[2:4], refs[4], refs[5]
    step = pl.program_id(0)
    frames = own_ref.shape[1]
    low = low_lanes((frames, BLK))
    even = low == (side[0] == 0)
    members = weight_ref.shape[0]
    side_rows = rows * members

    @pl.when(step == 0)
    def _():
        for at, far_ref in enumerate((far_a_ref, far_b_ref)):
            for m in range(far_ref.shape[0]):
                pair = far_ref[m].astype(jnp.float32)
                turned = half_turn(pair)
                first = 2 * (at * far_ref.shape[0] + m)
                partner[first] = jnp.where(low, pair, turned).astype(jnp.bfloat16)
                partner[first + 1] = jnp.where(low, turned, pair).astype(jnp.bfloat16)

    for member in range(members):
        for u in range(2):
            for h in range(HSTEP):
                for g in range(runs):
                    start = g * side_rows + member * rows
                    held[u, h, start:start + rows, :] = weight_ref[member, u, h, g]
    for m in range(HSTEP // 2):
        for u, source in enumerate((own_ref, partner)):
            pair = []
            for h in (2 * m, 2 * m + 1):
                at = [slots[u, (step * HSTEP + h) * runs + g] for g in range(runs)]
                left = jnp.concatenate(
                    [jnp.where(low, source[at[g]], source[at[g + 1]]) for g in range(0, runs, 2)], axis=1
                )
                pair.append(jnp.dot(left, held[u, h], preferred_element_type=jnp.float32))
            kept_refs[u][m] = jnp.where(even, pair[0], pair[1])
            sent_refs[u][m] = jnp.where(even, pair[1], pair[0]).astype(jnp.bfloat16)


def up_project(side, slots, own, far, weights):
    members, _, hidden_blocks, runs, rows, _ = weights.shape
    slots_all, frames, _ = own.shape
    out_spec = pl.BlockSpec((HSTEP // 2, frames, BLK), lambda i, *_: (i, 0, 0))
    return pl.pallas_call(
        functools.partial(up_kernel, runs=runs, rows=rows),
        grid_spec=pltpu.PrefetchScalarGridSpec(
            num_scalar_prefetch=2,
            grid=(hidden_blocks // HSTEP,),
            in_specs=[
                pl.BlockSpec((slots_all, frames, BLK), lambda i, *_: (0, 0, 0)),
                pl.BlockSpec((slots_all // 4, frames, BLK), lambda i, *_: (0, 0, 0)),
                pl.BlockSpec((slots_all // 4, frames, BLK), lambda i, *_: (0, 0, 0)),
                pl.BlockSpec((members, 2, HSTEP, runs, rows, BLK), lambda i, *_: (0, 0, i, 0, 0, 0)),
            ],
            out_specs=[out_spec] * 4,
            scratch_shapes=[
                pltpu.VMEM((slots_all, frames, BLK), jnp.bfloat16),
                pltpu.VMEM((2, HSTEP, runs * rows * members, BLK), jnp.bfloat16),
            ],
        ),
        out_shape=[pltpu.HBM((hidden_blocks // 2, frames, BLK), jnp.float32)] * 2
        + [pltpu.HBM((hidden_blocks // 2, frames, BLK), jnp.bfloat16)] * 2,
        compiler_params=pltpu.CompilerParams(vmem_limit_bytes=48 << 20),
        name="up_project",
    )(side, slots, *in_hbm([own]), *far, weights)


def down_kernel(side, which, wanted, *refs, utt, parts, runs, rows):
    refs = list(refs)
    step = pl.program_id(0)
    if parts:
        kept_refs, got_refs, refs = refs[:parts], refs[parts:2 * parts], refs[2 * parts:]
        weight_ref, out_ref, active_ref, held, total = refs
        per_part = pl.num_programs(0) // parts
        for p in range(parts):
            @pl.when(step // per_part == p)
            def _():
                before = kept_refs[p][...] + got_refs[p][...].astype(jnp.float32)
                active_ref[...] = (before / (1.0 + jnp.exp(-before))).astype(jnp.bfloat16)
    else:
        active_ref, weight_ref, out_ref, held, total = refs

    @pl.when(step == 0)
    def _():
        total[...] = jnp.zeros_like(total)
        held[...] = jnp.zeros_like(held)

    for h in range(HSTEP):
        top = HALF * (side[0] ^ (h % 2))
        for member in range(weight_ref.shape[0]):
            start = pl.multiple_of(member * rows + top, rows)
            for g in range(runs):
                at = (h % 2) * runs + g
                held[h // 2, pl.ds(start, rows), at * BLK:(at + 1) * BLK] = weight_ref[member, h, g]
    all_runs = 2 * runs
    for m in range(HSTEP // 2):
        product = jnp.dot(active_ref[m], held[m], preferred_element_type=jnp.float32)
        for odd in range(2):
            for g in range(runs):
                h = step * HSTEP + 2 * m + odd
                at = g * GROUP + wanted[utt, h * all_runs + which[0] * runs + g]
                lane = (odd * runs + g) * BLK
                total[at] += product[:, lane:lane + BLK]

    @pl.when(step == pl.num_programs(0) - 1)
    def _():
        out_ref[...] = total[...].astype(out_ref.dtype)


def down_project(side, which, wanted, sources, weights, utt, out_dtype):
    members, hidden_blocks, all_runs, rows, _ = weights.shape
    runs = all_runs // 2
    outs = runs * GROUP
    frames = sources[-1].shape[1]
    parts = len(sources) // 2
    steps = hidden_blocks // HSTEP
    per_part = steps // max(parts, 1)
    half_step = HSTEP // 2
    active_spec = pl.BlockSpec((half_step, frames, BLK), lambda i, *_: (i, 0, 0))
    if parts:
        source_specs = [
            pl.BlockSpec(
                (half_step, frames, BLK), lambda i, *_, p=p: (jnp.clip(i - p * per_part, 0, per_part - 1), 0, 0)
            )
            for p in range(parts)
        ] * 2
    else:
        source_specs = [active_spec]
    out_specs = [pl.BlockSpec((outs, frames, BLK), lambda i, *_: (0, 0, 0))]
    out_shape = [pltpu.HBM((outs, frames, BLK), out_dtype)]
    if parts:
        out_specs.append(active_spec)
        out_shape.append(pltpu.HBM((hidden_blocks // 2, frames, BLK), jnp.bfloat16))
    return pl.pallas_call(
        functools.partial(down_kernel, utt=utt, parts=parts, runs=runs, rows=rows),
        grid_spec=pltpu.PrefetchScalarGridSpec(
            num_scalar_prefetch=3,
            grid=(steps,),
            in_specs=source_specs
            + [
                pl.BlockSpec((members, HSTEP, runs, rows, BLK), lambda i, side, which, *_: (0, i, which[0], 0, 0))
            ],
            out_specs=out_specs,
            scratch_shapes=[
                pltpu.VMEM((half_step, BLK, 2 * runs * BLK), jnp.bfloat16),
                pltpu.VMEM((outs, frames, BLK), jnp.float32),
            ],
        ),
        out_shape=out_shape,
        compiler_params=pltpu.CompilerParams(vmem_limit_bytes=48 << 20),
        name=f"down_{utt}",
    )(side, which, wanted, *in_hbm(sources[:-parts] if parts else sources), *sources[len(sources) - parts:], weights)


def join_kernel(length, acoustic_ref, mine_ref, core_ref, side_ref, out_ref):
    frames = out_ref.shape[0]
    valid = lax.broadcasted_iota(jnp.int32, (frames, BLK), 0) < length[0]
    for d in range(mine_ref.shape[0]):
        lanes = slice(d * BLK, (d + 1) * BLK)
        feedfwd = mine_ref[d] + core_ref[d].astype(jnp.float32) + side_ref[d].astype(jnp.float32)
        summed = acoustic_ref[:, lanes].astype(jnp.float32) + feedfwd
        out_ref[:, lanes] = jnp.where(valid, summed, 0.0).astype(jnp.bfloat16)


def join(lengths, acoustic, mine, from_core, from_side):
    outs, frames, _ = mine.shape
    per = outs // 4
    block = pl.BlockSpec((per, frames, BLK), lambda i, *_: (i, 0, 0))
    flat = pl.BlockSpec((frames, per * BLK), lambda i, *_: (0, i))
    return pl.pallas_call(
        join_kernel,
        grid_spec=pltpu.PrefetchScalarGridSpec(
            num_scalar_prefetch=1, grid=(4,), in_specs=[flat, block, block, block], out_specs=flat
        ),
        out_shape=pltpu.HBM(acoustic.shape, jnp.bfloat16),
        name="join",
    )(lengths, acoustic, mine, from_core, from_side)


def swap(value, axis, size, step):
    return lax.ppermute(value, axis, [(i, i ^ step) for i in range(size)])


def in_hbm(values):
    return [pltpu.with_memory_space_constraint(value, pltpu.HBM) for value in values]


def split_body(acoustic, norm_gain, up_weight, down_weight, up_keep, down_keep, language, lengths, *, dp):
    frames, features = acoustic.shape
    nlangs, hidden_blocks, feat_blocks = up_keep.shape
    runs = feat_blocks // GROUP
    across = dp // 2
    members = list(range(across))
    here = lax.axis_index("dp").astype(jnp.int32)
    core = lax.axis_index("tensor").astype(jnp.int32)
    side = (here // across)[None]

    langs = language
    step = across
    while step != 0:
        langs = jnp.concatenate([langs, swap(langs, "dp", dp, step)])
        step = 1 if step == across else 2 * step
        step = 0 if step == across else step
    chooser = (langs[:, None] == jnp.arange(nlangs, dtype=jnp.int32)).astype(jnp.int32)
    wanted_up = jnp.einsum("nl,lhg->nhg", chooser, kept_within(up_keep))
    wanted_down = jnp.einsum("nl,lhg->nhg", chooser, kept_within(down_keep))
    up_own = wanted_up[:2] + jnp.arange(runs, dtype=jnp.int32) * GROUP
    slots = (up_own ^ (core * (feat_blocks // 2))).reshape(2, -1)
    wanted_up = wanted_up.reshape(2 * across, -1)
    wanted_down = wanted_down.reshape(2 * across, -1)
    place = (here % across)[None]
    peer = swap(acoustic, "tensor", 2, 1)
    gains = norm_gain.reshape(2, 1, features)
    gains = jnp.where(core == 0, gains, gains[::-1])
    near, own_far = norm_parts(side, acoustic, peer, gains)
    far = swap(own_far, "dp", dp, across)
    far = (far, swap(far, "tensor", 2, 1))

    groups = [[start + k for k in members] for start in (0, across)]

    def within_side(blocks):
        return lax.all_to_all(blocks, "dp", split_axis=0, concat_axis=0, axis_index_groups=groups, tiled=True)

    count = hidden_blocks // CHUNKS
    kept, crossed, after, got = ([], []), ([], []), in_hbm([own_far]), None
    for c in range(CHUNKS):
        (blocks,) = pick_blocks(up_weight, place, wanted_up, c * count, count, True, after)
        after = in_hbm([blocks])
        if got is not None:
            (blocks,) = gate([blocks], [got, *far])
            after = [got]
        got = within_side(blocks)
        span = slice(c * count * runs, (c + 1) * count * runs)
        kept_own, kept_far, sent_own, sent_far = up_project(side, slots[:, span], near, far, got)
        got_far = swap(sent_own, "dp", dp, across)
        (sent_far,) = gate([sent_far], [got_far])
        got_own = swap(sent_far, "dp", dp, across)
        for u, (mine, theirs) in enumerate(((kept_own, got_own), (kept_far, got_far))):
            kept[u].append(mine)
            crossed[u].append(theirs)
    own_blocks, far_blocks = pick_blocks(down_weight, place, wanted_down, 0, hidden_blocks, False, after)
    (far_blocks,) = gate([far_blocks], [got, *crossed[1][:-1]])
    far_down = within_side(far_blocks)
    (own_blocks,) = gate([own_blocks], [far_down, *crossed[1], *crossed[0][:-1]])
    own_down = within_side(own_blocks)
    rows_down = wanted_down[:2]

    def down(which, sources, weights, utt, dtype):
        return down_project(side, which, rows_down, sources, weights, utt, dtype)

    other_core = (1 - core)[None]
    this_core = core[None]
    for_peer, active_far = down(other_core, kept[1] + crossed[1], far_down, 1, jnp.bfloat16)
    from_peer = swap(for_peer, "tensor", 2, 1)
    (far_mine,) = down(this_core, [active_far], far_down, 1, jnp.float32)
    for_side = (far_mine + from_peer.astype(jnp.float32)).astype(jnp.bfloat16)
    from_side = swap(for_side, "dp", dp, across)
    own_peer, active_own = down(other_core, kept[0] + crossed[0], own_down, 0, jnp.bfloat16)
    from_core = swap(own_peer, "tensor", 2, 1)
    (own_mine,) = down(this_core, [active_own], own_down, 0, jnp.float32)
    return join(lengths, acoustic, own_mine, from_core, from_side)


def exchange_body(acoustic, norm_gain, up_weight, down_weight, up_keep, down_keep, language, lengths):
    frames = acoustic.shape[0]
    nlangs, hidden_blocks, feat_blocks = up_keep.shape
    block_side = BLK
    runs = feat_blocks // GROUP
    whole = lax.all_gather(acoustic, "tensor", axis=1, tiled=True)
    widened = whole.astype(jnp.float32)
    scale = lax.rsqrt(jnp.mean(widened * widened, axis=-1, keepdims=True) + 1e-06)
    normed = (widened * scale * norm_gain).astype(jnp.bfloat16)
    languages = lax.all_gather(language, "dp", axis=0, tiled=True)
    chooser = (languages[:, None] == jnp.arange(nlangs, dtype=jnp.int32)).astype(jnp.int32)
    own_pick = (language[0] == jnp.arange(nlangs, dtype=jnp.int32)).astype(jnp.int32)
    up_table = kept_index(up_keep)
    down_table = kept_index(down_keep)
    up_wanted = jnp.einsum("nl,lhg->nhg", chooser, up_table)
    down_wanted = jnp.einsum("nl,lhg->nhg", chooser, down_table)
    own_up = jnp.einsum("l,lhg->hg", own_pick, up_table)
    own_down = jnp.einsum("l,lhg->hg", own_pick, down_table)
    row_index = jnp.arange(hidden_blocks, dtype=jnp.int32)[None, :, None]
    send_up = up_weight[row_index, up_wanted]
    send_down = down_weight[row_index, down_wanted]
    got_up = lax.all_to_all(send_up, "dp", split_axis=0, concat_axis=3, tiled=True)
    got_down = None
    up_local = got_up[0].reshape(hidden_blocks, runs, block_side, block_side)
    chosen = normed.reshape(frames, feat_blocks, block_side)[:, own_up]
    before = jnp.einsum("thgi,hgij->thj", chosen, up_local, preferred_element_type=jnp.float32)
    active = jax.nn.silu(before).astype(jnp.bfloat16)
    got_down = lax.all_to_all(send_down, "dp", split_axis=0, concat_axis=3, tiled=True)
    down_local = got_down[0].reshape(hidden_blocks, runs, block_side, block_side)
    pieces = []
    for run_at in range(runs):
        contrib = jnp.einsum(
            "thi,hij->thj", active, down_local[:, run_at], preferred_element_type=jnp.float32
        )
        targets = run_at * GROUP + jnp.arange(GROUP, dtype=jnp.int32)
        onehot = (own_down[:, run_at, None] == targets).astype(jnp.float32)
        pieces.append(jnp.einsum("thj,hk->tkj", contrib, onehot, precision=lax.Precision.HIGHEST))
    partial_value = jnp.concatenate(pieces, axis=1).reshape(frames, feat_blocks * block_side)
    feedfwd = lax.psum_scatter(
        partial_value.astype(jnp.bfloat16), "tensor", scatter_dimension=1, tiled=True
    ).astype(jnp.float32)
    valid = (jnp.arange(frames, dtype=jnp.int32) < lengths[0]).astype(jnp.float32)
    return ((acoustic.astype(jnp.float32) + feedfwd) * valid[:, None]).astype(jnp.bfloat16)


def solution(mesh):
    in_specs = (
        P(("parts", "dp"), "tensor"),
        P(),
        P("tensor", None, "dp"),
        P("tensor", None, "dp"),
        P(None, "tensor", None),
        P(None, "tensor", None),
        P(("parts", "dp")),
        P(("parts", "dp")),
    )
    out_specs = P(("parts", "dp"), "tensor")
    dp = mesh.shape["dp"]
    rows = BLK // dp
    whole_tiles = mesh.shape["tensor"] == 2 and dp & (dp - 1) == 0 and dp > 1 and rows % 16 == 0
    body = functools.partial(split_body, dp=dp) if whole_tiles else exchange_body
    return jax.shard_map(body, mesh=mesh, in_specs=in_specs, out_specs=out_specs, check_vma=False)
```

```python
import functools

import jax
import jax.numpy as jnp
from jax import lax
from jax.experimental import pallas as pl
from jax.experimental.pallas import tpu as pltpu
from jax.sharding import PartitionSpec as P

BLK = 128
HALF = BLK // 2
GROUP = 8
HSTEP = 8
CHUNKS = 2
PSTEP = 4


def kept_within(keep_mask):
    nlangs, hidden_blocks, feat_blocks = keep_mask.shape
    runs = feat_blocks // GROUP
    picks = jnp.arange(GROUP, dtype=jnp.int32)
    return jnp.sum(keep_mask.reshape(nlangs, hidden_blocks, runs, GROUP) * picks, axis=-1)


def kept_index(keep_mask):
    within = kept_within(keep_mask)
    return within + jnp.arange(within.shape[-1], dtype=jnp.int32) * GROUP


def low_lanes(shape):
    return lax.broadcasted_iota(jnp.int32, shape, len(shape) - 1) < HALF


def half_turn(value):
    return pltpu.roll(value, HALF, value.ndim - 1)


def norm_kernel(side, own_ref, peer_ref, gain_ref, near_ref, far_ref):
    frames, features = own_ref.shape
    slots = features // BLK

    def square(ref):
        total = jnp.zeros((frames, BLK), jnp.float32)
        for d in range(slots):
            wide = ref[:, d * BLK:(d + 1) * BLK].astype(jnp.float32)
            total = total + wide * wide
        return total

    mean = jnp.sum(square(own_ref) + square(peer_ref), axis=-1, keepdims=True) / (2 * features)
    scale = lax.rsqrt(mean + 1e-06)
    low = low_lanes((frames, BLK))
    near_low = low == (side[0] == 0)
    for at, ref in enumerate((own_ref, peer_ref)):
        for d in range(0, slots, 2):
            far = []
            for e in (d, d + 1):
                lanes = slice(e * BLK, (e + 1) * BLK)
                gain = gain_ref[at, :, lanes]
                rounded = (ref[:, lanes].astype(jnp.float32) * scale * gain).astype(jnp.bfloat16).astype(jnp.float32)
                turned = half_turn(rounded)
                near_ref[at * slots + e] = jnp.where(near_low, rounded, turned).astype(jnp.bfloat16)
                far.append(jnp.where(near_low, turned, rounded))
            if at == 0:
                far_ref[d // 2] = jnp.where(low, far[0], far[1]).astype(jnp.bfloat16)


def norm_parts(side, own, peer, gains):
    frames, features = own.shape
    slots = 2 * features // BLK
    return pl.pallas_call(
        norm_kernel,
        grid_spec=pltpu.PrefetchScalarGridSpec(
            num_scalar_prefetch=1,
            grid=(1,),
            in_specs=[
                pl.BlockSpec((frames, features), lambda i, *_: (0, 0)),
                pl.BlockSpec((frames, features), lambda i, *_: (0, 0)),
                pl.BlockSpec((2, 1, features), lambda i, *_: (0, 0, 0)),
            ],
            out_specs=[
                pl.BlockSpec((slots, frames, BLK), lambda i, *_: (0, 0, 0)),
                pl.BlockSpec((slots // 4, frames, BLK), lambda i, *_: (0, 0, 0)),
            ],
        ),
        out_shape=[
            pltpu.HBM((slots, frames, BLK), jnp.bfloat16),
            pltpu.HBM((slots // 4, frames, BLK), jnp.bfloat16),
        ],
        name="norm_parts",
    )(side, own, peer, gains)


def pick_kernel(place, wanted, weight_ref, *refs, rows, runs, after):
    out_refs, spread = refs[after:-1], refs[-1]
    step = pl.program_id(0)
    for h in range(HSTEP):
        for row in range(rows):
            tile = weight_ref[h, :, row * BLK:(row + 1) * BLK].astype(jnp.float32)
            for g in range(runs):
                spread[h * runs + g, row * GROUP:(row + 1) * GROUP, :] = tile[g * GROUP:(g + 1) * GROUP]
    for member in range(wanted.shape[0] // 2):
        pair = 2 * (place[0] ^ member)
        for u in range(2):
            for h in range(HSTEP):
                for g in range(runs):
                    at = wanted[pair + u, (step * HSTEP + h) * runs + g]
                    block = spread[h * runs + g, pl.ds(at, rows, stride=GROUP), :]
                    out_refs[u][member, h, g] = block.astype(jnp.bfloat16)


def pick_blocks(weight, place, wanted, after=()):
    hidden_blocks, feat_blocks, width = weight.shape
    rows = width // BLK
    runs = feat_blocks // GROUP
    members = wanted.shape[0] // 2
    shape = (members, hidden_blocks, runs, rows, BLK)
    out_spec = pl.BlockSpec((members, HSTEP, runs, rows, BLK), lambda i, *_: (0, i, 0, 0, 0))
    return pl.pallas_call(
        functools.partial(pick_kernel, rows=rows, runs=runs, after=len(after)),
        grid_spec=pltpu.PrefetchScalarGridSpec(
            num_scalar_prefetch=2,
            grid=(hidden_blocks // HSTEP,),
            in_specs=[pl.BlockSpec((HSTEP, feat_blocks, width), lambda i, *_: (i, 0, 0))]
            + [corner(value) for value in after],
            out_specs=[out_spec] * 2,
            scratch_shapes=[pltpu.VMEM((HSTEP * runs, rows * GROUP, BLK), jnp.float32)],
        ),
        out_shape=[pltpu.HBM(shape, jnp.bfloat16)] * 2,
        compiler_params=pltpu.CompilerParams(vmem_limit_bytes=48 << 20),
        name="pick_down",
    )(place, wanted, *in_hbm([weight]), *after)


def pick_both_kernel(at_home, wanted, own_ref, other_ref, *refs, rows, runs, base, half, after):
    out_ref, spread = refs[after], refs[after + 1]
    step = pl.program_id(0)
    for s, ref in enumerate((own_ref, other_ref)):
        for h in range(PSTEP):
            for row in range(rows):
                tile = ref[h, :, row * BLK:(row + 1) * BLK].astype(jnp.float32)
                for g in range(runs):
                    spread[s, h * runs + g, row * GROUP:(row + 1) * GROUP, :] = tile[g * GROUP:(g + 1) * GROUP]
    first = base + at_home[2] * half + step * PSTEP
    places = [pl.multiple_of(group * rows, rows) for group in (at_home[1], 1 - at_home[1])]
    for member in range(wanted.shape[0] // 2):
        pair = 2 * (at_home[0] ^ member)
        for u in range(2):
            for h in range(PSTEP):
                for g in range(runs):
                    at = wanted[pair + u, (first + h) * runs + g]
                    for s in range(2):
                        block = spread[s, h * runs + g, pl.ds(at, rows, stride=GROUP), :]
                        if h % 2:
                            block = half_turn(block)
                        out_ref[member, u, h, g, pl.ds(places[s], rows), :] = block.astype(jnp.bfloat16)


def pick_both(weight, other, at_home, wanted, base, after=()):
    _, feat_blocks, width = weight.shape
    half = other.shape[0]
    rows = width // BLK
    runs = feat_blocks // GROUP
    members = wanted.shape[0] // 2
    per_half = half // PSTEP
    first = base // PSTEP
    return pl.pallas_call(
        functools.partial(pick_both_kernel, rows=rows, runs=runs, base=base, half=half, after=len(after)),
        grid_spec=pltpu.PrefetchScalarGridSpec(
            num_scalar_prefetch=2,
            grid=(per_half,),
            in_specs=[
                pl.BlockSpec(
                    (PSTEP, feat_blocks, width), lambda i, at_home, wanted: (first + at_home[2] * per_half + i, 0, 0)
                ),
                pl.BlockSpec((PSTEP, feat_blocks, width), lambda i, *_: (i, 0, 0)),
            ]
            + [corner(value) for value in after],
            out_specs=pl.BlockSpec((members, 2, PSTEP, runs, 2 * rows, BLK), lambda i, *_: (0, 0, i, 0, 0, 0)),
            scratch_shapes=[pltpu.VMEM((2, PSTEP * runs, rows * GROUP, BLK), jnp.float32)],
        ),
        out_shape=pltpu.HBM((members, 2, half, runs, 2 * rows, BLK), jnp.bfloat16),
        compiler_params=pltpu.CompilerParams(vmem_limit_bytes=48 << 20),
        name="pick_both",
    )(at_home, wanted, *in_hbm([weight]), other, *after)


def corner(value):
    zeros = (0,) * value.ndim
    return pl.BlockSpec((1,) * (value.ndim - 2) + (16, BLK), lambda i, *_: zeros)


def gate_kernel(*refs):
    del refs


def gate(values, after):
    anywhere = pl.BlockSpec(memory_space=pl.ANY)
    return pl.pallas_call(
        gate_kernel,
        grid=(1,),
        in_specs=[anywhere] * len(values) + [corner(value) for value in after],
        out_specs=[anywhere] * len(values),
        out_shape=[pltpu.HBM(value.shape, value.dtype) for value in values],
        input_output_aliases={i: i for i in range(len(values))},
        name="gate",
    )(*in_hbm(values), *after)


def up_kernel(side, slots, own_ref, far_a_ref, far_b_ref, weight_ref, *refs, runs, rows, half):
    kept_refs, sent_refs, partner, held = refs[:2], refs[2:4], refs[4], refs[5]
    step = pl.program_id(0)
    frames = own_ref.shape[1]
    low = low_lanes((frames, BLK))
    even = low == (side[0] == 0)
    members, half_step = weight_ref.shape[0], weight_ref.shape[2]
    side_rows = 4 * rows

    @pl.when(step == 0)
    def _():
        for at, far_ref in enumerate((far_a_ref, far_b_ref)):
            for m in range(far_ref.shape[0]):
                pair = far_ref[m].astype(jnp.float32)
                turned = half_turn(pair)
                first = 2 * (at * far_ref.shape[0] + m)
                partner[first] = jnp.where(low, pair, turned).astype(jnp.bfloat16)
                partner[first + 1] = jnp.where(low, turned, pair).astype(jnp.bfloat16)

    for member in range(members):
        part, place = divmod(member, 2)
        for u in range(2):
            for h in range(half_step):
                for g in range(runs):
                    for group in range(2):
                        start = g * side_rows + (2 * group + place) * rows
                        held[u, part * half_step + h, start:start + rows, :] = weight_ref[
                            member, u, h, g, group * rows:(group + 1) * rows
                        ]
    for m in range(half_step):
        part, within = divmod(m, half_step // 2)
        for u, source in enumerate((own_ref, partner)):
            pair = []
            for h in (2 * m, 2 * m + 1):
                hidden = part * half + step * half_step + h % half_step
                at = [slots[u, hidden * runs + g] for g in range(runs)]
                left = jnp.concatenate(
                    [jnp.where(low, source[at[g]], source[at[g + 1]]) for g in range(0, runs, 2)], axis=1
                )
                pair.append(jnp.dot(left, held[u, h], preferred_element_type=jnp.float32))
            kept_refs[u][part, within] = jnp.where(even, pair[0], pair[1])
            sent_refs[u][part, within] = jnp.where(even, pair[1], pair[0]).astype(jnp.bfloat16)


def up_project(side, slots, own, far, weights):
    members, _, half, runs, both, _ = weights.shape
    rows = both // 2
    half_step = HSTEP // 2
    slots_all, frames, _ = own.shape
    out_spec = pl.BlockSpec((2, half_step // 2, frames, BLK), lambda i, *_: (0, i, 0, 0))
    out_dims = (2, half // 2, frames, BLK)
    out = pl.pallas_call(
        functools.partial(up_kernel, runs=runs, rows=rows, half=half),
        grid_spec=pltpu.PrefetchScalarGridSpec(
            num_scalar_prefetch=2,
            grid=(half // half_step,),
            in_specs=[
                pl.BlockSpec((slots_all, frames, BLK), lambda i, *_: (0, 0, 0)),
                pl.BlockSpec((slots_all // 4, frames, BLK), lambda i, *_: (0, 0, 0)),
                pl.BlockSpec((slots_all // 4, frames, BLK), lambda i, *_: (0, 0, 0)),
                pl.BlockSpec((members, 2, half_step, runs, both, BLK), lambda i, *_: (0, 0, i, 0, 0, 0)),
            ],
            out_specs=[out_spec] * 4,
            scratch_shapes=[
                pltpu.VMEM((slots_all, frames, BLK), jnp.bfloat16),
                pltpu.VMEM((2, HSTEP, runs * rows * 4, BLK), jnp.bfloat16),
            ],
        ),
        out_shape=[pltpu.HBM(out_dims, jnp.float32)] * 2 + [pltpu.HBM(out_dims, jnp.bfloat16)] * 2,
        compiler_params=pltpu.CompilerParams(vmem_limit_bytes=48 << 20),
        name="up_project",
    )(side, slots, *in_hbm([own]), *far, weights)
    return [value.reshape(half, frames, BLK) for value in out]


def down_kernel(side, which, wanted, *refs, utt, parts, runs, rows):
    refs = list(refs)
    step = pl.program_id(0)
    if parts:
        kept_refs, got_refs, refs = refs[:parts], refs[parts:2 * parts], refs[2 * parts:]
        weight_ref, out_ref, active_ref, held, total = refs
        per_part = pl.num_programs(0) // parts
        for p in range(parts):
            @pl.when(step // per_part == p)
            def _():
                before = kept_refs[p][...] + got_refs[p][...].astype(jnp.float32)
                active_ref[...] = (before / (1.0 + jnp.exp(-before))).astype(jnp.bfloat16)
    else:
        active_ref, weight_ref, out_ref, held, total = refs

    @pl.when(step == 0)
    def _():
        total[...] = jnp.zeros_like(total)
        held[...] = jnp.zeros_like(held)

    for h in range(HSTEP):
        top = HALF * (side[0] ^ (h % 2))
        for member in range(weight_ref.shape[0]):
            start = pl.multiple_of(member * rows + top, rows)
            for g in range(runs):
                at = (h % 2) * runs + g
                held[h // 2, pl.ds(start, rows), at * BLK:(at + 1) * BLK] = weight_ref[member, h, g]
    all_runs = 2 * runs
    for m in range(HSTEP // 2):
        product = jnp.dot(active_ref[m], held[m], preferred_element_type=jnp.float32)
        for odd in range(2):
            for g in range(runs):
                h = step * HSTEP + 2 * m + odd
                at = g * GROUP + wanted[utt, h * all_runs + which[0] * runs + g]
                lane = (odd * runs + g) * BLK
                total[at] += product[:, lane:lane + BLK]

    @pl.when(step == pl.num_programs(0) - 1)
    def _():
        out_ref[...] = total[...].astype(out_ref.dtype)


def down_project(side, which, wanted, sources, weights, utt, out_dtype):
    members, hidden_blocks, all_runs, rows, _ = weights.shape
    runs = all_runs // 2
    outs = runs * GROUP
    frames = sources[-1].shape[1]
    parts = len(sources) // 2
    steps = hidden_blocks // HSTEP
    per_part = steps // max(parts, 1)
    half_step = HSTEP // 2
    active_spec = pl.BlockSpec((half_step, frames, BLK), lambda i, *_: (i, 0, 0))
    if parts:
        source_specs = [
            pl.BlockSpec(
                (half_step, frames, BLK), lambda i, *_, p=p: (jnp.clip(i - p * per_part, 0, per_part - 1), 0, 0)
            )
            for p in range(parts)
        ] * 2
    else:
        source_specs = [active_spec]
    out_specs = [pl.BlockSpec((outs, frames, BLK), lambda i, *_: (0, 0, 0))]
    out_shape = [pltpu.HBM((outs, frames, BLK), out_dtype)]
    if parts:
        out_specs.append(active_spec)
        out_shape.append(pltpu.HBM((hidden_blocks // 2, frames, BLK), jnp.bfloat16))
    return pl.pallas_call(
        functools.partial(down_kernel, utt=utt, parts=parts, runs=runs, rows=rows),
        grid_spec=pltpu.PrefetchScalarGridSpec(
            num_scalar_prefetch=3,
            grid=(steps,),
            in_specs=source_specs
            + [
                pl.BlockSpec((members, HSTEP, runs, rows, BLK), lambda i, side, which, *_: (0, i, which[0], 0, 0))
            ],
            out_specs=out_specs,
            scratch_shapes=[
                pltpu.VMEM((half_step, BLK, 2 * runs * BLK), jnp.bfloat16),
                pltpu.VMEM((outs, frames, BLK), jnp.float32),
            ],
        ),
        out_shape=out_shape,
        compiler_params=pltpu.CompilerParams(vmem_limit_bytes=48 << 20),
        name=f"down_{utt}",
    )(side, which, wanted, *in_hbm(sources[:-parts] if parts else sources), *sources[len(sources) - parts:], weights)


def join_kernel(length, acoustic_ref, mine_ref, core_ref, side_ref, out_ref):
    frames = out_ref.shape[0]
    valid = lax.broadcasted_iota(jnp.int32, (frames, BLK), 0) < length[0]
    for d in range(mine_ref.shape[0]):
        lanes = slice(d * BLK, (d + 1) * BLK)
        feedfwd = mine_ref[d] + core_ref[d].astype(jnp.float32) + side_ref[d].astype(jnp.float32)
        summed = acoustic_ref[:, lanes].astype(jnp.float32) + feedfwd
        out_ref[:, lanes] = jnp.where(valid, summed, 0.0).astype(jnp.bfloat16)


def join(lengths, acoustic, mine, from_core, from_side):
    outs, frames, _ = mine.shape
    per = outs // 4
    block = pl.BlockSpec((per, frames, BLK), lambda i, *_: (i, 0, 0))
    flat = pl.BlockSpec((frames, per * BLK), lambda i, *_: (0, i))
    return pl.pallas_call(
        join_kernel,
        grid_spec=pltpu.PrefetchScalarGridSpec(
            num_scalar_prefetch=1, grid=(4,), in_specs=[flat, block, block, block], out_specs=flat
        ),
        out_shape=pltpu.HBM(acoustic.shape, jnp.bfloat16),
        name="join",
    )(lengths, acoustic, mine, from_core, from_side)


def swap(value, axis, size, step):
    return lax.ppermute(value, axis, [(i, i ^ step) for i in range(size)])


def in_hbm(values):
    return [pltpu.with_memory_space_constraint(value, pltpu.HBM) for value in values]


def split_body(acoustic, norm_gain, up_weight, down_weight, up_keep, down_keep, language, lengths, *, dp):
    frames, features = acoustic.shape
    nlangs, hidden_blocks, feat_blocks = up_keep.shape
    runs = feat_blocks // GROUP
    across = dp // 2
    members = list(range(across))
    here = lax.axis_index("dp").astype(jnp.int32)
    core = lax.axis_index("tensor").astype(jnp.int32)
    side = (here // across)[None]

    part = lax.axis_index("parts").astype(jnp.int32)
    count = hidden_blocks // CHUNKS
    half = count // 2
    other_rows, raw = [], None
    for c in range(CHUNKS):
        mine = lax.dynamic_slice_in_dim(up_weight, c * count + part * half, half, 0)
        if raw is not None:
            (mine,) = gate([mine], [raw])
        raw = swap(mine, "dp", dp, 2)
        other_rows.append(raw)

    langs = language
    for step in (across, 1):
        langs = jnp.concatenate([langs, swap(langs, "dp", dp, step)])

    def wanted_of(langs, table):
        chooser = (langs[:, None] == jnp.arange(nlangs, dtype=jnp.int32)).astype(jnp.int32)
        return jnp.einsum("nl,lhg->nhg", chooser, table)

    wanted_up = wanted_of(jnp.concatenate([langs, swap(langs, "parts", 2, 1)]), kept_within(up_keep))
    wanted_down = wanted_of(jnp.concatenate([langs, swap(langs, "dp", dp, 2)]), kept_within(down_keep))
    up_own = wanted_up[:2] + jnp.arange(runs, dtype=jnp.int32) * GROUP
    slots = (up_own ^ (core * (feat_blocks // 2))).reshape(2, -1)
    wanted_up = wanted_up.reshape(2 * across, -1)
    wanted_down = wanted_down.reshape(2 * across, -1)
    place = (here % across)[None]
    at_home = jnp.stack([2 * part + here % 2, here % across // 2, part])
    peer = swap(acoustic, "tensor", 2, 1)
    gains = norm_gain.reshape(2, 1, features)
    gains = jnp.where(core == 0, gains, gains[::-1])
    near, own_far = norm_parts(side, acoustic, peer, gains)
    (own_far,) = gate([own_far], [other_rows[0]])
    far = swap(own_far, "dp", dp, across)
    far = (far, swap(far, "tensor", 2, 1))

    groups = [[start + k for k in members] for start in (0, across)]

    def within_side(blocks):
        return lax.all_to_all(blocks, "dp", split_axis=0, concat_axis=0, axis_index_groups=groups, tiled=True)

    trades = [[p * dp + 2 * z + x for p in range(2) for x in range(2)] for z in range(dp // 2)]

    def traded(blocks):
        return lax.all_to_all(
            blocks, ("parts", "dp"), split_axis=0, concat_axis=0, axis_index_groups=trades, tiled=True
        )

    kept, crossed, got, after = ([], []), ([], []), None, ()
    for c in range(CHUNKS):
        blocks = pick_both(up_weight, other_rows[c], at_home, wanted_up, c * count, after)
        after = in_hbm([blocks])
        if got is not None:
            (blocks,) = gate([blocks], [got])
        got = traded(blocks)
        span = slice(c * count * runs, (c + 1) * count * runs)
        kept_own, kept_far, sent_own, sent_far = up_project(side, slots[:, span], near, far, got)
        got_far = swap(sent_own, "dp", dp, across)
        (sent_far,) = gate([sent_far], [got_far])
        got_own = swap(sent_far, "dp", dp, across)
        for u, (mine, theirs) in enumerate(((kept_own, got_own), (kept_far, got_far))):
            kept[u].append(mine)
            crossed[u].append(theirs)
    own_blocks, far_blocks = pick_blocks(down_weight, place, wanted_down, [other_rows[-1]])
    (far_blocks,) = gate([far_blocks], [got, *crossed[1][:-1], *crossed[0][:-1]])
    far_down = within_side(far_blocks)
    (own_blocks,) = gate([own_blocks], [far_down, *crossed[1]])
    own_down = within_side(own_blocks)
    rows_down = wanted_down[:2]

    def down(which, sources, weights, utt, dtype):
        return down_project(side, which, rows_down, sources, weights, utt, dtype)

    other_core = (1 - core)[None]
    this_core = core[None]
    for_peer, active_far = down(other_core, kept[1] + crossed[1], far_down, 1, jnp.bfloat16)
    from_peer = swap(for_peer, "tensor", 2, 1)
    (far_mine,) = down(this_core, [active_far], far_down, 1, jnp.float32)
    for_side = (far_mine + from_peer.astype(jnp.float32)).astype(jnp.bfloat16)
    from_side = swap(for_side, "dp", dp, across)
    own_peer, active_own = down(other_core, kept[0] + crossed[0], own_down, 0, jnp.bfloat16)
    from_core = swap(own_peer, "tensor", 2, 1)
    (own_mine,) = down(this_core, [active_own], own_down, 0, jnp.float32)
    return join(lengths, acoustic, own_mine, from_core, from_side)


def exchange_body(acoustic, norm_gain, up_weight, down_weight, up_keep, down_keep, language, lengths):
    frames = acoustic.shape[0]
    nlangs, hidden_blocks, feat_blocks = up_keep.shape
    block_side = BLK
    runs = feat_blocks // GROUP
    whole = lax.all_gather(acoustic, "tensor", axis=1, tiled=True)
    widened = whole.astype(jnp.float32)
    scale = lax.rsqrt(jnp.mean(widened * widened, axis=-1, keepdims=True) + 1e-06)
    normed = (widened * scale * norm_gain).astype(jnp.bfloat16)
    languages = lax.all_gather(language, "dp", axis=0, tiled=True)
    chooser = (languages[:, None] == jnp.arange(nlangs, dtype=jnp.int32)).astype(jnp.int32)
    own_pick = (language[0] == jnp.arange(nlangs, dtype=jnp.int32)).astype(jnp.int32)
    up_table = kept_index(up_keep)
    down_table = kept_index(down_keep)
    up_wanted = jnp.einsum("nl,lhg->nhg", chooser, up_table)
    down_wanted = jnp.einsum("nl,lhg->nhg", chooser, down_table)
    own_up = jnp.einsum("l,lhg->hg", own_pick, up_table)
    own_down = jnp.einsum("l,lhg->hg", own_pick, down_table)
    row_index = jnp.arange(hidden_blocks, dtype=jnp.int32)[None, :, None]
    send_up = up_weight[row_index, up_wanted]
    send_down = down_weight[row_index, down_wanted]
    got_up = lax.all_to_all(send_up, "dp", split_axis=0, concat_axis=3, tiled=True)
    got_down = None
    up_local = got_up[0].reshape(hidden_blocks, runs, block_side, block_side)
    chosen = normed.reshape(frames, feat_blocks, block_side)[:, own_up]
    before = jnp.einsum("thgi,hgij->thj", chosen, up_local, preferred_element_type=jnp.float32)
    active = jax.nn.silu(before).astype(jnp.bfloat16)
    got_down = lax.all_to_all(send_down, "dp", split_axis=0, concat_axis=3, tiled=True)
    down_local = got_down[0].reshape(hidden_blocks, runs, block_side, block_side)
    pieces = []
    for run_at in range(runs):
        contrib = jnp.einsum(
            "thi,hij->thj", active, down_local[:, run_at], preferred_element_type=jnp.float32
        )
        targets = run_at * GROUP + jnp.arange(GROUP, dtype=jnp.int32)
        onehot = (own_down[:, run_at, None] == targets).astype(jnp.float32)
        pieces.append(jnp.einsum("thj,hk->tkj", contrib, onehot, precision=lax.Precision.HIGHEST))
    partial_value = jnp.concatenate(pieces, axis=1).reshape(frames, feat_blocks * block_side)
    feedfwd = lax.psum_scatter(
        partial_value.astype(jnp.bfloat16), "tensor", scatter_dimension=1, tiled=True
    ).astype(jnp.float32)
    valid = (jnp.arange(frames, dtype=jnp.int32) < lengths[0]).astype(jnp.float32)
    return ((acoustic.astype(jnp.float32) + feedfwd) * valid[:, None]).astype(jnp.bfloat16)


def solution(mesh):
    in_specs = (
        P(("parts", "dp"), "tensor"),
        P(),
        P("tensor", None, "dp"),
        P("tensor", None, "dp"),
        P(None, "tensor", None),
        P(None, "tensor", None),
        P(("parts", "dp")),
        P(("parts", "dp")),
    )
    out_specs = P(("parts", "dp"), "tensor")
    dp = mesh.shape["dp"]
    in_pairs = mesh.shape["tensor"] == 2 and mesh.shape["parts"] == 2 and dp == 8
    body = functools.partial(split_body, dp=dp) if in_pairs else exchange_body
    return jax.shard_map(body, mesh=mesh, in_specs=in_specs, out_specs=out_specs, check_vma=False)
```

```python
import functools

import jax
import jax.numpy as jnp
from jax import lax
from jax.experimental import pallas as pl
from jax.experimental.pallas import tpu as pltpu
from jax.sharding import PartitionSpec as P

BLK = 128
HALF = BLK // 2
GROUP = 8
HSTEP = 8
CHUNKS = 2


def kept_within(keep_mask):
    nlangs, hidden_blocks, feat_blocks = keep_mask.shape
    runs = feat_blocks // GROUP
    picks = jnp.arange(GROUP, dtype=jnp.int32)
    return jnp.sum(keep_mask.reshape(nlangs, hidden_blocks, runs, GROUP) * picks, axis=-1)


def kept_index(keep_mask):
    within = kept_within(keep_mask)
    return within + jnp.arange(within.shape[-1], dtype=jnp.int32) * GROUP


def low_lanes(shape):
    return lax.broadcasted_iota(jnp.int32, shape, len(shape) - 1) < HALF


def half_turn(value):
    return pltpu.roll(value, HALF, value.ndim - 1)


def norm_kernel(side, own_ref, peer_ref, gain_ref, near_ref, far_ref):
    frames, features = own_ref.shape
    slots = features // BLK

    def square(ref):
        total = jnp.zeros((frames, BLK), jnp.float32)
        for d in range(slots):
            wide = ref[:, d * BLK:(d + 1) * BLK].astype(jnp.float32)
            total = total + wide * wide
        return total

    mean = jnp.sum(square(own_ref) + square(peer_ref), axis=-1, keepdims=True) / (2 * features)
    scale = lax.rsqrt(mean + 1e-06)
    low = low_lanes((frames, BLK))
    near_low = low == (side[0] == 0)
    for at, ref in enumerate((own_ref, peer_ref)):
        for d in range(0, slots, 2):
            far = []
            for e in (d, d + 1):
                lanes = slice(e * BLK, (e + 1) * BLK)
                gain = gain_ref[at, :, lanes]
                rounded = (ref[:, lanes].astype(jnp.float32) * scale * gain).astype(jnp.bfloat16).astype(jnp.float32)
                turned = half_turn(rounded)
                near_ref[at * slots + e] = jnp.where(near_low, rounded, turned).astype(jnp.bfloat16)
                far.append(jnp.where(near_low, turned, rounded))
            if at == 0:
                far_ref[d // 2] = jnp.where(low, far[0], far[1]).astype(jnp.bfloat16)


def norm_parts(side, own, peer, gains):
    frames, features = own.shape
    slots = 2 * features // BLK
    return pl.pallas_call(
        norm_kernel,
        grid_spec=pltpu.PrefetchScalarGridSpec(
            num_scalar_prefetch=1,
            grid=(1,),
            in_specs=[
                pl.BlockSpec((frames, features), lambda i, *_: (0, 0)),
                pl.BlockSpec((frames, features), lambda i, *_: (0, 0)),
                pl.BlockSpec((2, 1, features), lambda i, *_: (0, 0, 0)),
            ],
            out_specs=[
                pl.BlockSpec((slots, frames, BLK), lambda i, *_: (0, 0, 0)),
                pl.BlockSpec((slots // 4, frames, BLK), lambda i, *_: (0, 0, 0)),
            ],
        ),
        out_shape=[
            pltpu.HBM((slots, frames, BLK), jnp.bfloat16),
            pltpu.HBM((slots // 4, frames, BLK), jnp.bfloat16),
        ],
        name="norm_parts",
    )(side, own, peer, gains)


def pick_kernel(place, wanted, weight_ref, *refs, rows, runs, base, up, after):
    out_refs, spread = refs[after:-1], refs[-1]
    step = pl.program_id(0) + base
    for h in range(HSTEP):
        for row in range(rows):
            tile = weight_ref[h, :, row * BLK:(row + 1) * BLK].astype(jnp.float32)
            for g in range(runs):
                spread[h * runs + g, row * GROUP:(row + 1) * GROUP, :] = tile[g * GROUP:(g + 1) * GROUP]
    for member in range(wanted.shape[0] // 2):
        pair = 2 * member if up else 2 * (place[0] ^ member)
        for u in range(2):
            for h in range(HSTEP):
                for g in range(runs):
                    at = wanted[pair + u, (step * HSTEP + h) * runs + g]
                    block = spread[h * runs + g, pl.ds(at, rows, stride=GROUP), :]
                    if up and h % 2:
                        block = half_turn(block)
                    block = block.astype(jnp.bfloat16)
                    if up:
                        out_refs[member][u, h, g] = block
                    else:
                        out_refs[u][member, h, g] = block


def pick_blocks(weight, place, wanted, first, count, up, after=()):
    _, feat_blocks, width = weight.shape
    rows = width // BLK
    runs = feat_blocks // GROUP
    base = first // HSTEP
    members = wanted.shape[0] // 2
    outs, lead = (members, 2) if up else (2, members)
    return pl.pallas_call(
        functools.partial(pick_kernel, rows=rows, runs=runs, base=base, up=up, after=len(after)),
        grid_spec=pltpu.PrefetchScalarGridSpec(
            num_scalar_prefetch=2,
            grid=(count // HSTEP,),
            in_specs=[pl.BlockSpec((HSTEP, feat_blocks, width), lambda i, *_: (i + base, 0, 0))]
            + [corner(value) for value in after],
            out_specs=[pl.BlockSpec((lead, HSTEP, runs, rows, BLK), lambda i, *_: (0, i, 0, 0, 0))] * outs,
            scratch_shapes=[pltpu.VMEM((HSTEP * runs, rows * GROUP, BLK), jnp.float32)],
        ),
        out_shape=[pltpu.HBM((lead, count, runs, rows, BLK), jnp.bfloat16)] * outs,
        compiler_params=pltpu.CompilerParams(vmem_limit_bytes=48 << 20),
        name="pick_up" if up else "pick_down",
    )(place, wanted, *in_hbm([weight]), *after)


def corner(value):
    zeros = (0,) * value.ndim
    return pl.BlockSpec((1,) * (value.ndim - 2) + (16, BLK), lambda i, *_: zeros)


def gate_kernel(*refs):
    del refs


def gate(values, after):
    anywhere = pl.BlockSpec(memory_space=pl.ANY)
    return pl.pallas_call(
        gate_kernel,
        grid=(1,),
        in_specs=[anywhere] * len(values) + [corner(value) for value in after],
        out_specs=[anywhere] * len(values),
        out_shape=[pltpu.HBM(value.shape, value.dtype) for value in values],
        input_output_aliases={i: i for i in range(len(values))},
        name="gate",
    )(*in_hbm(values), *after)


def up_kernel(side, place, slots, own_ref, far_a_ref, far_b_ref, *refs, runs, rows):
    weight_refs, refs = refs[:-6], refs[-6:]
    kept_refs, sent_refs, partner, held = refs[:2], refs[2:4], refs[4], refs[5]
    step = pl.program_id(0)
    frames = own_ref.shape[1]
    low = low_lanes((frames, BLK))
    even = low == (side[0] == 0)
    side_rows = rows * len(weight_refs)

    @pl.when(step == 0)
    def _():
        for at, far_ref in enumerate((far_a_ref, far_b_ref)):
            for m in range(far_ref.shape[0]):
                pair = far_ref[m].astype(jnp.float32)
                turned = half_turn(pair)
                first = 2 * (at * far_ref.shape[0] + m)
                partner[first] = jnp.where(low, pair, turned).astype(jnp.bfloat16)
                partner[first + 1] = jnp.where(low, turned, pair).astype(jnp.bfloat16)

    for k, ref in enumerate(weight_refs):
        start = pl.multiple_of(place[k] * rows, rows)
        for u in range(2):
            for h in range(HSTEP):
                for g in range(runs):
                    held[u, h, pl.ds(start + g * side_rows, rows), :] = ref[u, h, g]
    for m in range(HSTEP // 2):
        for u, source in enumerate((own_ref, partner)):
            pair = []
            for h in (2 * m, 2 * m + 1):
                at = [slots[u, (step * HSTEP + h) * runs + g] for g in range(runs)]
                left = jnp.concatenate(
                    [jnp.where(low, source[at[g]], source[at[g + 1]]) for g in range(0, runs, 2)], axis=1
                )
                pair.append(jnp.dot(left, held[u, h], preferred_element_type=jnp.float32))
            kept_refs[u][m] = jnp.where(even, pair[0], pair[1])
            sent_refs[u][m] = jnp.where(even, pair[1], pair[0]).astype(jnp.bfloat16)


def up_project(side, place, slots, own, far, weights):
    _, hidden_blocks, runs, rows, _ = weights[0].shape
    slots_all, frames, _ = own.shape
    out_spec = pl.BlockSpec((HSTEP // 2, frames, BLK), lambda i, *_: (i, 0, 0))
    return pl.pallas_call(
        functools.partial(up_kernel, runs=runs, rows=rows),
        grid_spec=pltpu.PrefetchScalarGridSpec(
            num_scalar_prefetch=3,
            grid=(hidden_blocks // HSTEP,),
            in_specs=[
                pl.BlockSpec((slots_all, frames, BLK), lambda i, *_: (0, 0, 0)),
                pl.BlockSpec((slots_all // 4, frames, BLK), lambda i, *_: (0, 0, 0)),
                pl.BlockSpec((slots_all // 4, frames, BLK), lambda i, *_: (0, 0, 0)),
            ]
            + [pl.BlockSpec((2, HSTEP, runs, rows, BLK), lambda i, *_: (0, i, 0, 0, 0))] * len(weights),
            out_specs=[out_spec] * 4,
            scratch_shapes=[
                pltpu.VMEM((slots_all, frames, BLK), jnp.bfloat16),
                pltpu.VMEM((2, HSTEP, runs * rows * len(weights), BLK), jnp.bfloat16),
            ],
        ),
        out_shape=[pltpu.HBM((hidden_blocks // 2, frames, BLK), jnp.float32)] * 2
        + [pltpu.HBM((hidden_blocks // 2, frames, BLK), jnp.bfloat16)] * 2,
        compiler_params=pltpu.CompilerParams(vmem_limit_bytes=48 << 20),
        name="up_project",
    )(side, place, slots, own, *far, *weights)


def down_kernel(side, which, wanted, *refs, utt, parts, runs, rows):
    refs = list(refs)
    step = pl.program_id(0)
    if parts:
        kept_refs, got_refs, refs = refs[:parts], refs[parts:2 * parts], refs[2 * parts:]
        weight_ref, out_ref, active_ref, held, total = refs
        per_part = pl.num_programs(0) // parts
        for p in range(parts):
            @pl.when(step // per_part == p)
            def _():
                before = kept_refs[p][...] + got_refs[p][...].astype(jnp.float32)
                active_ref[...] = (before / (1.0 + jnp.exp(-before))).astype(jnp.bfloat16)
    else:
        active_ref, weight_ref, out_ref, held, total = refs

    @pl.when(step == 0)
    def _():
        total[...] = jnp.zeros_like(total)
        held[...] = jnp.zeros_like(held)

    for h in range(HSTEP):
        top = HALF * (side[0] ^ (h % 2))
        for member in range(weight_ref.shape[0]):
            start = pl.multiple_of(member * rows + top, rows)
            for g in range(runs):
                at = (h % 2) * runs + g
                held[h // 2, pl.ds(start, rows), at * BLK:(at + 1) * BLK] = weight_ref[member, h, g]
    all_runs = 2 * runs
    for m in range(HSTEP // 2):
        product = jnp.dot(active_ref[m], held[m], preferred_element_type=jnp.float32)
        for odd in range(2):
            for g in range(runs):
                h = step * HSTEP + 2 * m + odd
                at = g * GROUP + wanted[utt, h * all_runs + which[0] * runs + g]
                lane = (odd * runs + g) * BLK
                total[at] += product[:, lane:lane + BLK]

    @pl.when(step == pl.num_programs(0) - 1)
    def _():
        out_ref[...] = total[...].astype(out_ref.dtype)


def down_project(side, which, wanted, sources, weights, utt, out_dtype):
    members, hidden_blocks, all_runs, rows, _ = weights.shape
    runs = all_runs // 2
    outs = runs * GROUP
    frames = sources[-1].shape[1]
    parts = len(sources) // 2
    steps = hidden_blocks // HSTEP
    per_part = steps // max(parts, 1)
    half_step = HSTEP // 2
    active_spec = pl.BlockSpec((half_step, frames, BLK), lambda i, *_: (i, 0, 0))
    if parts:
        source_specs = [
            pl.BlockSpec(
                (half_step, frames, BLK), lambda i, *_, p=p: (jnp.clip(i - p * per_part, 0, per_part - 1), 0, 0)
            )
            for p in range(parts)
        ] * 2
    else:
        source_specs = [active_spec]
    out_specs = [pl.BlockSpec((outs, frames, BLK), lambda i, *_: (0, 0, 0))]
    out_shape = [pltpu.HBM((outs, frames, BLK), out_dtype)]
    if parts:
        out_specs.append(active_spec)
        out_shape.append(pltpu.HBM((hidden_blocks // 2, frames, BLK), jnp.bfloat16))
    return pl.pallas_call(
        functools.partial(down_kernel, utt=utt, parts=parts, runs=runs, rows=rows),
        grid_spec=pltpu.PrefetchScalarGridSpec(
            num_scalar_prefetch=3,
            grid=(steps,),
            in_specs=source_specs
            + [
                pl.BlockSpec((members, HSTEP, runs, rows, BLK), lambda i, side, which, *_: (0, i, which[0], 0, 0))
            ],
            out_specs=out_specs,
            scratch_shapes=[
                pltpu.VMEM((half_step, BLK, 2 * runs * BLK), jnp.bfloat16),
                pltpu.VMEM((outs, frames, BLK), jnp.float32),
            ],
        ),
        out_shape=out_shape,
        compiler_params=pltpu.CompilerParams(vmem_limit_bytes=48 << 20),
        name=f"down_{utt}",
    )(side, which, wanted, *in_hbm(sources[:-parts] if parts else sources), *sources[len(sources) - parts:], weights)


def join_kernel(length, acoustic_ref, mine_ref, core_ref, side_ref, out_ref):
    frames = out_ref.shape[0]
    valid = lax.broadcasted_iota(jnp.int32, (frames, BLK), 0) < length[0]
    for d in range(mine_ref.shape[0]):
        lanes = slice(d * BLK, (d + 1) * BLK)
        feedfwd = mine_ref[d] + core_ref[d].astype(jnp.float32) + side_ref[d].astype(jnp.float32)
        summed = acoustic_ref[:, lanes].astype(jnp.float32) + feedfwd
        out_ref[:, lanes] = jnp.where(valid, summed, 0.0).astype(jnp.bfloat16)


def join(lengths, acoustic, mine, from_core, from_side):
    outs, frames, _ = mine.shape
    per = outs // 4
    block = pl.BlockSpec((per, frames, BLK), lambda i, *_: (i, 0, 0))
    flat = pl.BlockSpec((frames, per * BLK), lambda i, *_: (0, i))
    return pl.pallas_call(
        join_kernel,
        grid_spec=pltpu.PrefetchScalarGridSpec(
            num_scalar_prefetch=1, grid=(4,), in_specs=[flat, block, block, block], out_specs=flat
        ),
        out_shape=pltpu.HBM(acoustic.shape, jnp.bfloat16),
        name="join",
    )(lengths, acoustic, mine, from_core, from_side)


def swap(value, axis, size, step):
    return lax.ppermute(value, axis, [(i, i ^ step) for i in range(size)])


def in_hbm(values):
    return [pltpu.with_memory_space_constraint(value, pltpu.HBM) for value in values]


def split_body(acoustic, norm_gain, up_weight, down_weight, up_keep, down_keep, language, lengths, *, dp):
    frames, features = acoustic.shape
    nlangs, hidden_blocks, feat_blocks = up_keep.shape
    runs = feat_blocks // GROUP
    across = dp // 2
    members = list(range(across))
    here = lax.axis_index("dp").astype(jnp.int32)
    core = lax.axis_index("tensor").astype(jnp.int32)
    side = (here // across)[None]

    langs = language
    step = across
    while step != 0:
        langs = jnp.concatenate([langs, swap(langs, "dp", dp, step)])
        step = 1 if step == across else 2 * step
        step = 0 if step == across else step
    chooser = (langs[:, None] == jnp.arange(nlangs, dtype=jnp.int32)).astype(jnp.int32)
    wanted_up = jnp.einsum("nl,lhg->nhg", chooser, kept_within(up_keep))
    wanted_down = jnp.einsum("nl,lhg->nhg", chooser, kept_within(down_keep))
    up_own = wanted_up[:2] + jnp.arange(runs, dtype=jnp.int32) * GROUP
    slots = (up_own ^ (core * (feat_blocks // 2))).reshape(2, -1)
    wanted_up = wanted_up.reshape(2 * across, -1)
    wanted_down = wanted_down.reshape(2 * across, -1)
    place = jnp.stack([(here ^ k) % across for k in members])
    peer = swap(acoustic, "tensor", 2, 1)
    gains = norm_gain.reshape(2, 1, features)
    gains = jnp.where(core == 0, gains, gains[::-1])
    near, own_far = norm_parts(side, acoustic, peer, gains)
    far = swap(own_far, "dp", dp, across)
    far = (far, swap(far, "tensor", 2, 1))

    groups = [[start + k for k in members] for start in (0, across)]

    def by_distance(blocks):
        return [blocks[0]] + [swap(blocks[k], "dp", dp, k) for k in members[1:]]

    def in_order(blocks):
        return lax.all_to_all(blocks, "dp", split_axis=0, concat_axis=0, axis_index_groups=groups, tiled=True)

    count = hidden_blocks // CHUNKS
    kept, crossed, after = ([], []), ([], []), in_hbm([own_far])
    for c in range(CHUNKS):
        blocks = pick_blocks(up_weight, place, wanted_up, c * count, count, True, after)
        after = [*in_hbm(blocks[:1]), far[0]]
        got = by_distance(blocks)
        span = slice(c * count * runs, (c + 1) * count * runs)
        kept_own, kept_far, sent_own, sent_far = up_project(side, place, slots[:, span], near, far, got)
        got_far = swap(sent_own, "dp", dp, across)
        got_own = swap(sent_far, "dp", dp, across)
        for u, (mine, theirs) in enumerate(((kept_own, got_own), (kept_far, got_far))):
            kept[u].append(mine)
            crossed[u].append(theirs)
    own_blocks, far_blocks = pick_blocks(
        down_weight, place, wanted_down, 0, hidden_blocks, False, in_hbm(kept[0][:1])
    )
    (far_blocks,) = gate([far_blocks], [*crossed[1][:1], *got[1:]])
    far_down = in_order(far_blocks)
    (own_blocks,) = gate([own_blocks], [far_down, crossed[1][-1], crossed[0][0]])
    own_down = in_order(own_blocks)
    rows_down = wanted_down[:2]

    def down(which, sources, weights, utt, dtype):
        return down_project(side, which, rows_down, sources, weights, utt, dtype)

    other_core = (1 - core)[None]
    this_core = core[None]
    for_peer, active_far = down(other_core, kept[1] + crossed[1], far_down, 1, jnp.bfloat16)
    from_peer = swap(for_peer, "tensor", 2, 1)
    (far_mine,) = down(this_core, [active_far], far_down, 1, jnp.float32)
    for_side = (far_mine + from_peer.astype(jnp.float32)).astype(jnp.bfloat16)
    from_side = swap(for_side, "dp", dp, across)
    own_peer, active_own = down(other_core, kept[0] + crossed[0], own_down, 0, jnp.bfloat16)
    from_core = swap(own_peer, "tensor", 2, 1)
    (own_mine,) = down(this_core, [active_own], own_down, 0, jnp.float32)
    return join(lengths, acoustic, own_mine, from_core, from_side)


def exchange_body(acoustic, norm_gain, up_weight, down_weight, up_keep, down_keep, language, lengths):
    frames = acoustic.shape[0]
    nlangs, hidden_blocks, feat_blocks = up_keep.shape
    block_side = BLK
    runs = feat_blocks // GROUP
    whole = lax.all_gather(acoustic, "tensor", axis=1, tiled=True)
    widened = whole.astype(jnp.float32)
    scale = lax.rsqrt(jnp.mean(widened * widened, axis=-1, keepdims=True) + 1e-06)
    normed = (widened * scale * norm_gain).astype(jnp.bfloat16)
    languages = lax.all_gather(language, "dp", axis=0, tiled=True)
    chooser = (languages[:, None] == jnp.arange(nlangs, dtype=jnp.int32)).astype(jnp.int32)
    own_pick = (language[0] == jnp.arange(nlangs, dtype=jnp.int32)).astype(jnp.int32)
    up_table = kept_index(up_keep)
    down_table = kept_index(down_keep)
    up_wanted = jnp.einsum("nl,lhg->nhg", chooser, up_table)
    down_wanted = jnp.einsum("nl,lhg->nhg", chooser, down_table)
    own_up = jnp.einsum("l,lhg->hg", own_pick, up_table)
    own_down = jnp.einsum("l,lhg->hg", own_pick, down_table)
    row_index = jnp.arange(hidden_blocks, dtype=jnp.int32)[None, :, None]
    send_up = up_weight[row_index, up_wanted]
    send_down = down_weight[row_index, down_wanted]
    got_up = lax.all_to_all(send_up, "dp", split_axis=0, concat_axis=3, tiled=True)
    got_down = None
    up_local = got_up[0].reshape(hidden_blocks, runs, block_side, block_side)
    chosen = normed.reshape(frames, feat_blocks, block_side)[:, own_up]
    before = jnp.einsum("thgi,hgij->thj", chosen, up_local, preferred_element_type=jnp.float32)
    active = jax.nn.silu(before).astype(jnp.bfloat16)
    got_down = lax.all_to_all(send_down, "dp", split_axis=0, concat_axis=3, tiled=True)
    down_local = got_down[0].reshape(hidden_blocks, runs, block_side, block_side)
    pieces = []
    for run_at in range(runs):
        contrib = jnp.einsum(
            "thi,hij->thj", active, down_local[:, run_at], preferred_element_type=jnp.float32
        )
        targets = run_at * GROUP + jnp.arange(GROUP, dtype=jnp.int32)
        onehot = (own_down[:, run_at, None] == targets).astype(jnp.float32)
        pieces.append(jnp.einsum("thj,hk->tkj", contrib, onehot, precision=lax.Precision.HIGHEST))
    partial_value = jnp.concatenate(pieces, axis=1).reshape(frames, feat_blocks * block_side)
    feedfwd = lax.psum_scatter(
        partial_value.astype(jnp.bfloat16), "tensor", scatter_dimension=1, tiled=True
    ).astype(jnp.float32)
    valid = (jnp.arange(frames, dtype=jnp.int32) < lengths[0]).astype(jnp.float32)
    return ((acoustic.astype(jnp.float32) + feedfwd) * valid[:, None]).astype(jnp.bfloat16)


def solution(mesh):
    in_specs = (
        P(("parts", "dp"), "tensor"),
        P(),
        P("tensor", None, "dp"),
        P("tensor", None, "dp"),
        P(None, "tensor", None),
        P(None, "tensor", None),
        P(("parts", "dp")),
        P(("parts", "dp")),
    )
    out_specs = P(("parts", "dp"), "tensor")
    dp = mesh.shape["dp"]
    rows = BLK // dp
    whole_tiles = mesh.shape["tensor"] == 2 and dp & (dp - 1) == 0 and dp > 1 and rows % 16 == 0
    body = functools.partial(split_body, dp=dp) if whole_tiles else exchange_body
    return jax.shard_map(body, mesh=mesh, in_specs=in_specs, out_specs=out_specs, check_vma=False)
```

```python
import functools

import jax
import jax.numpy as jnp
from jax import lax
from jax.experimental import pallas as pl
from jax.experimental.pallas import tpu as pltpu
from jax.sharding import PartitionSpec as P

BLK = 128
HALF = BLK // 2
GROUP = 8
HSTEP = 8
CHUNKS = 2


def kept_within(keep_mask):
    nlangs, hidden_blocks, feat_blocks = keep_mask.shape
    runs = feat_blocks // GROUP
    picks = jnp.arange(GROUP, dtype=jnp.int32)
    return jnp.sum(keep_mask.reshape(nlangs, hidden_blocks, runs, GROUP) * picks, axis=-1)


def kept_index(keep_mask):
    within = kept_within(keep_mask)
    return within + jnp.arange(within.shape[-1], dtype=jnp.int32) * GROUP


def low_lanes(shape):
    return lax.broadcasted_iota(jnp.int32, shape, len(shape) - 1) < HALF


def half_turn(value):
    return pltpu.roll(value, HALF, value.ndim - 1)


def norm_kernel(side, own_ref, peer_ref, gain_ref, near_ref, far_ref):
    frames, features = own_ref.shape
    slots = features // BLK

    def square(ref):
        total = jnp.zeros((frames, BLK), jnp.float32)
        for d in range(slots):
            wide = ref[:, d * BLK:(d + 1) * BLK].astype(jnp.float32)
            total = total + wide * wide
        return total

    mean = jnp.sum(square(own_ref) + square(peer_ref), axis=-1, keepdims=True) / (2 * features)
    scale = lax.rsqrt(mean + 1e-06)
    low = low_lanes((frames, BLK))
    near_low = low == (side[0] == 0)
    for at, ref in enumerate((own_ref, peer_ref)):
        for d in range(0, slots, 2):
            far = []
            for e in (d, d + 1):
                lanes = slice(e * BLK, (e + 1) * BLK)
                gain = gain_ref[at, :, lanes]
                rounded = (ref[:, lanes].astype(jnp.float32) * scale * gain).astype(jnp.bfloat16).astype(jnp.float32)
                turned = half_turn(rounded)
                near_ref[at * slots + e] = jnp.where(near_low, rounded, turned).astype(jnp.bfloat16)
                far.append(jnp.where(near_low, turned, rounded))
            if at == 0:
                far_ref[d // 2] = jnp.where(low, far[0], far[1]).astype(jnp.bfloat16)


def norm_parts(side, own, peer, gains):
    frames, features = own.shape
    slots = 2 * features // BLK
    return pl.pallas_call(
        norm_kernel,
        grid_spec=pltpu.PrefetchScalarGridSpec(
            num_scalar_prefetch=1,
            grid=(1,),
            in_specs=[
                pl.BlockSpec((frames, features), lambda i, *_: (0, 0)),
                pl.BlockSpec((frames, features), lambda i, *_: (0, 0)),
                pl.BlockSpec((2, 1, features), lambda i, *_: (0, 0, 0)),
            ],
            out_specs=[
                pl.BlockSpec((slots, frames, BLK), lambda i, *_: (0, 0, 0)),
                pl.BlockSpec((slots // 4, frames, BLK), lambda i, *_: (0, 0, 0)),
            ],
        ),
        out_shape=[
            pltpu.HBM((slots, frames, BLK), jnp.bfloat16),
            pltpu.HBM((slots // 4, frames, BLK), jnp.bfloat16),
        ],
        name="norm_parts",
    )(side, own, peer, gains)


def pick_kernel(place, wanted, weight_ref, *refs, rows, runs, base, up, after):
    out_refs, spread = refs[after:-1], refs[-1]
    step = pl.program_id(0) + base
    for h in range(HSTEP):
        for row in range(rows):
            tile = weight_ref[h, :, row * BLK:(row + 1) * BLK].astype(jnp.float32)
            for g in range(runs):
                spread[h * runs + g, row * GROUP:(row + 1) * GROUP, :] = tile[g * GROUP:(g + 1) * GROUP]
    for member in range(wanted.shape[0] // 2):
        pair = 2 * member if up else 2 * (place[0] ^ member)
        for u in range(2):
            for h in range(HSTEP):
                for g in range(runs):
                    at = wanted[pair + u, (step * HSTEP + h) * runs + g]
                    block = spread[h * runs + g, pl.ds(at, rows, stride=GROUP), :]
                    if up and h % 2:
                        block = half_turn(block)
                    block = block.astype(jnp.bfloat16)
                    if up:
                        out_refs[member][u, h, g] = block
                    else:
                        out_refs[u][member, h, g] = block


def pick_blocks(weight, place, wanted, first, count, up, after=()):
    _, feat_blocks, width = weight.shape
    rows = width // BLK
    runs = feat_blocks // GROUP
    base = first // HSTEP
    members = wanted.shape[0] // 2
    outs, lead = (members, 2) if up else (2, members)
    return pl.pallas_call(
        functools.partial(pick_kernel, rows=rows, runs=runs, base=base, up=up, after=len(after)),
        grid_spec=pltpu.PrefetchScalarGridSpec(
            num_scalar_prefetch=2,
            grid=(count // HSTEP,),
            in_specs=[pl.BlockSpec((HSTEP, feat_blocks, width), lambda i, *_: (i + base, 0, 0))]
            + [corner(value) for value in after],
            out_specs=[pl.BlockSpec((lead, HSTEP, runs, rows, BLK), lambda i, *_: (0, i, 0, 0, 0))] * outs,
            scratch_shapes=[pltpu.VMEM((HSTEP * runs, rows * GROUP, BLK), jnp.float32)],
        ),
        out_shape=[pltpu.HBM((lead, count, runs, rows, BLK), jnp.bfloat16)] * outs,
        compiler_params=pltpu.CompilerParams(vmem_limit_bytes=48 << 20),
        name="pick_up" if up else "pick_down",
    )(place, wanted, *in_hbm([weight]), *after)


def corner(value):
    zeros = (0,) * value.ndim
    return pl.BlockSpec((1,) * (value.ndim - 2) + (16, BLK), lambda i, *_: zeros)


def gate_kernel(*refs):
    del refs


def gate(values, after):
    anywhere = pl.BlockSpec(memory_space=pl.ANY)
    return pl.pallas_call(
        gate_kernel,
        grid=(1,),
        in_specs=[anywhere] * len(values) + [corner(value) for value in after],
        out_specs=[anywhere] * len(values),
        out_shape=[pltpu.HBM(value.shape, value.dtype) for value in values],
        input_output_aliases={i: i for i in range(len(values))},
        name="gate",
    )(*in_hbm(values), *after)


def up_kernel(side, place, slots, own_ref, far_a_ref, far_b_ref, *refs, runs, rows):
    weight_refs, refs = refs[:-6], refs[-6:]
    kept_refs, sent_refs, partner, held = refs[:2], refs[2:4], refs[4], refs[5]
    step = pl.program_id(0)
    frames = own_ref.shape[1]
    low = low_lanes((frames, BLK))
    even = low == (side[0] == 0)
    side_rows = rows * len(weight_refs)

    @pl.when(step == 0)
    def _():
        for at, far_ref in enumerate((far_a_ref, far_b_ref)):
            for m in range(far_ref.shape[0]):
                pair = far_ref[m].astype(jnp.float32)
                turned = half_turn(pair)
                first = 2 * (at * far_ref.shape[0] + m)
                partner[first] = jnp.where(low, pair, turned).astype(jnp.bfloat16)
                partner[first + 1] = jnp.where(low, turned, pair).astype(jnp.bfloat16)

    for k, ref in enumerate(weight_refs):
        start = pl.multiple_of(place[k] * rows, rows)
        for u in range(2):
            for h in range(HSTEP):
                for g in range(runs):
                    held[u, h, pl.ds(start + g * side_rows, rows), :] = ref[u, h, g]
    for m in range(HSTEP // 2):
        for u, source in enumerate((own_ref, partner)):
            pair = []
            for h in (2 * m, 2 * m + 1):
                at = [slots[u, (step * HSTEP + h) * runs + g] for g in range(runs)]
                left = jnp.concatenate(
                    [jnp.where(low, source[at[g]], source[at[g + 1]]) for g in range(0, runs, 2)], axis=1
                )
                pair.append(jnp.dot(left, held[u, h], preferred_element_type=jnp.float32))
            kept_refs[u][m] = jnp.where(even, pair[0], pair[1])
            sent_refs[u][m] = jnp.where(even, pair[1], pair[0]).astype(jnp.bfloat16)


def up_project(side, place, slots, own, far, weights):
    _, hidden_blocks, runs, rows, _ = weights[0].shape
    slots_all, frames, _ = own.shape
    out_spec = pl.BlockSpec((HSTEP // 2, frames, BLK), lambda i, *_: (i, 0, 0))
    return pl.pallas_call(
        functools.partial(up_kernel, runs=runs, rows=rows),
        grid_spec=pltpu.PrefetchScalarGridSpec(
            num_scalar_prefetch=3,
            grid=(hidden_blocks // HSTEP,),
            in_specs=[
                pl.BlockSpec((slots_all, frames, BLK), lambda i, *_: (0, 0, 0)),
                pl.BlockSpec((slots_all // 4, frames, BLK), lambda i, *_: (0, 0, 0)),
                pl.BlockSpec((slots_all // 4, frames, BLK), lambda i, *_: (0, 0, 0)),
            ]
            + [pl.BlockSpec((2, HSTEP, runs, rows, BLK), lambda i, *_: (0, i, 0, 0, 0))] * len(weights),
            out_specs=[out_spec] * 4,
            scratch_shapes=[
                pltpu.VMEM((slots_all, frames, BLK), jnp.bfloat16),
                pltpu.VMEM((2, HSTEP, runs * rows * len(weights), BLK), jnp.bfloat16),
            ],
        ),
        out_shape=[pltpu.HBM((hidden_blocks // 2, frames, BLK), jnp.float32)] * 2
        + [pltpu.HBM((hidden_blocks // 2, frames, BLK), jnp.bfloat16)] * 2,
        compiler_params=pltpu.CompilerParams(vmem_limit_bytes=48 << 20),
        name="up_project",
    )(side, place, slots, own, *far, *weights)


def down_kernel(side, which, wanted, *refs, utt, parts, runs, rows):
    refs = list(refs)
    step = pl.program_id(0)
    if parts:
        kept_refs, got_refs, refs = refs[:parts], refs[parts:2 * parts], refs[2 * parts:]
        weight_ref, out_ref, active_ref, held, total = refs
        per_part = pl.num_programs(0) // parts
        for p in range(parts):
            @pl.when(step // per_part == p)
            def _():
                before = kept_refs[p][...] + got_refs[p][...].astype(jnp.float32)
                active_ref[...] = (before / (1.0 + jnp.exp(-before))).astype(jnp.bfloat16)
    else:
        active_ref, weight_ref, out_ref, held, total = refs

    @pl.when(step == 0)
    def _():
        total[...] = jnp.zeros_like(total)
        held[...] = jnp.zeros_like(held)

    for h in range(HSTEP):
        top = HALF * (side[0] ^ (h % 2))
        for member in range(weight_ref.shape[0]):
            start = pl.multiple_of(member * rows + top, rows)
            for g in range(runs):
                at = (h % 2) * runs + g
                held[h // 2, pl.ds(start, rows), at * BLK:(at + 1) * BLK] = weight_ref[member, h, g]
    all_runs = 2 * runs
    for m in range(HSTEP // 2):
        product = jnp.dot(active_ref[m], held[m], preferred_element_type=jnp.float32)
        for odd in range(2):
            for g in range(runs):
                h = step * HSTEP + 2 * m + odd
                at = g * GROUP + wanted[utt, h * all_runs + which[0] * runs + g]
                lane = (odd * runs + g) * BLK
                total[at] += product[:, lane:lane + BLK]

    @pl.when(step == pl.num_programs(0) - 1)
    def _():
        out_ref[...] = total[...].astype(out_ref.dtype)


def down_project(side, which, wanted, sources, weights, utt, out_dtype):
    members, hidden_blocks, all_runs, rows, _ = weights.shape
    runs = all_runs // 2
    outs = runs * GROUP
    frames = sources[-1].shape[1]
    parts = len(sources) // 2
    steps = hidden_blocks // HSTEP
    per_part = steps // max(parts, 1)
    half_step = HSTEP // 2
    active_spec = pl.BlockSpec((half_step, frames, BLK), lambda i, *_: (i, 0, 0))
    if parts:
        source_specs = [
            pl.BlockSpec(
                (half_step, frames, BLK), lambda i, *_, p=p: (jnp.clip(i - p * per_part, 0, per_part - 1), 0, 0)
            )
            for p in range(parts)
        ] * 2
    else:
        source_specs = [active_spec]
    out_specs = [pl.BlockSpec((outs, frames, BLK), lambda i, *_: (0, 0, 0))]
    out_shape = [pltpu.HBM((outs, frames, BLK), out_dtype)]
    if parts:
        out_specs.append(active_spec)
        out_shape.append(pltpu.HBM((hidden_blocks // 2, frames, BLK), jnp.bfloat16))
    return pl.pallas_call(
        functools.partial(down_kernel, utt=utt, parts=parts, runs=runs, rows=rows),
        grid_spec=pltpu.PrefetchScalarGridSpec(
            num_scalar_prefetch=3,
            grid=(steps,),
            in_specs=source_specs
            + [
                pl.BlockSpec((members, HSTEP, runs, rows, BLK), lambda i, side, which, *_: (0, i, which[0], 0, 0))
            ],
            out_specs=out_specs,
            scratch_shapes=[
                pltpu.VMEM((half_step, BLK, 2 * runs * BLK), jnp.bfloat16),
                pltpu.VMEM((outs, frames, BLK), jnp.float32),
            ],
        ),
        out_shape=out_shape,
        compiler_params=pltpu.CompilerParams(vmem_limit_bytes=48 << 20),
        name=f"down_{utt}",
    )(side, which, wanted, *in_hbm(sources[:-parts] if parts else sources), *sources[len(sources) - parts:], weights)


def swap(value, axis, size, step):
    return lax.ppermute(value, axis, [(i, i ^ step) for i in range(size)])


def in_hbm(values):
    return [pltpu.with_memory_space_constraint(value, pltpu.HBM) for value in values]


def split_body(acoustic, norm_gain, up_weight, down_weight, up_keep, down_keep, language, lengths, *, dp):
    frames, features = acoustic.shape
    nlangs, hidden_blocks, feat_blocks = up_keep.shape
    runs = feat_blocks // GROUP
    across = dp // 2
    members = list(range(across))
    here = lax.axis_index("dp").astype(jnp.int32)
    core = lax.axis_index("tensor").astype(jnp.int32)
    side = (here // across)[None]

    peer = swap(acoustic, "tensor", 2, 1)
    gains = norm_gain.reshape(2, 1, features)
    gains = jnp.where(core == 0, gains, gains[::-1])
    near, own_far = norm_parts(side, acoustic, peer, gains)
    far = swap(own_far, "dp", dp, across)
    far = (far, swap(far, "tensor", 2, 1))
    langs = jnp.concatenate([language, swap(language, "dp", dp, across)])
    (langs,) = gate([langs], in_hbm([own_far]))
    step = 1
    while step != across:
        langs = jnp.concatenate([langs, swap(langs, "dp", dp, step)])
        step = 2 * step
    chooser = (langs[:, None] == jnp.arange(nlangs, dtype=jnp.int32)).astype(jnp.int32)
    wanted_up = jnp.einsum("nl,lhg->nhg", chooser, kept_within(up_keep))
    wanted_down = jnp.einsum("nl,lhg->nhg", chooser, kept_within(down_keep))
    up_own = wanted_up[:2] + jnp.arange(runs, dtype=jnp.int32) * GROUP
    slots = (up_own ^ (core * (feat_blocks // 2))).reshape(2, -1)
    wanted_up = wanted_up.reshape(2 * across, -1)
    wanted_down = wanted_down.reshape(2 * across, -1)
    place = jnp.stack([(here ^ k) % across for k in members])

    groups = [[start + k for k in members] for start in (0, across)]

    def by_distance(blocks):
        return [blocks[0]] + [swap(blocks[k], "dp", dp, k) for k in members[1:]]

    def in_order(blocks):
        return lax.all_to_all(blocks, "dp", split_axis=0, concat_axis=0, axis_index_groups=groups, tiled=True)

    count = hidden_blocks // CHUNKS
    kept, crossed, after = ([], []), ([], []), in_hbm([own_far])
    for c in range(CHUNKS):
        blocks = pick_blocks(up_weight, place, wanted_up, c * count, count, True, after)
        after = [*in_hbm(blocks[:1]), far[0]]
        got = by_distance(blocks)
        span = slice(c * count * runs, (c + 1) * count * runs)
        kept_own, kept_far, sent_own, sent_far = up_project(side, place, slots[:, span], near, far, got)
        got_far = swap(sent_own, "dp", dp, across)
        got_own = swap(sent_far, "dp", dp, across)
        for u, (mine, theirs) in enumerate(((kept_own, got_own), (kept_far, got_far))):
            kept[u].append(mine)
            crossed[u].append(theirs)
    own_blocks, far_blocks = pick_blocks(
        down_weight, place, wanted_down, 0, hidden_blocks, False, in_hbm(kept[0][:1])
    )
    (far_blocks,) = gate([far_blocks], [*crossed[1][:1], *got[1:]])
    far_down = in_order(far_blocks)
    (own_blocks,) = gate([own_blocks], [far_down, crossed[1][-1], crossed[0][0]])
    own_down = in_order(own_blocks)
    rows_down = wanted_down[:2]

    def down(which, sources, weights, utt, dtype):
        return down_project(side, which, rows_down, sources, weights, utt, dtype)

    other_core = (1 - core)[None]
    this_core = core[None]
    for_peer, active_far = down(other_core, kept[1] + crossed[1], far_down, 1, jnp.bfloat16)
    from_peer = swap(for_peer, "tensor", 2, 1)
    (far_mine,) = down(this_core, [active_far], far_down, 1, jnp.float32)
    for_side = (far_mine + from_peer.astype(jnp.float32)).astype(jnp.bfloat16)
    from_side = swap(for_side, "dp", dp, across)
    own_peer, active_own = down(other_core, kept[0] + crossed[0], own_down, 0, jnp.bfloat16)
    from_core = swap(own_peer, "tensor", 2, 1)
    (own_mine,) = down(this_core, [active_own], own_down, 0, jnp.float32)
    feedfwd = own_mine + from_core.astype(jnp.float32) + from_side.astype(jnp.float32)
    feedfwd = feedfwd.transpose(1, 0, 2).reshape(frames, features)
    valid = jnp.arange(frames, dtype=jnp.int32)[:, None] < lengths[0]
    return jnp.where(valid, acoustic.astype(jnp.float32) + feedfwd, 0.0).astype(jnp.bfloat16)


def exchange_body(acoustic, norm_gain, up_weight, down_weight, up_keep, down_keep, language, lengths):
    frames = acoustic.shape[0]
    nlangs, hidden_blocks, feat_blocks = up_keep.shape
    block_side = BLK
    runs = feat_blocks // GROUP
    whole = lax.all_gather(acoustic, "tensor", axis=1, tiled=True)
    widened = whole.astype(jnp.float32)
    scale = lax.rsqrt(jnp.mean(widened * widened, axis=-1, keepdims=True) + 1e-06)
    normed = (widened * scale * norm_gain).astype(jnp.bfloat16)
    languages = lax.all_gather(language, "dp", axis=0, tiled=True)
    chooser = (languages[:, None] == jnp.arange(nlangs, dtype=jnp.int32)).astype(jnp.int32)
    own_pick = (language[0] == jnp.arange(nlangs, dtype=jnp.int32)).astype(jnp.int32)
    up_table = kept_index(up_keep)
    down_table = kept_index(down_keep)
    up_wanted = jnp.einsum("nl,lhg->nhg", chooser, up_table)
    down_wanted = jnp.einsum("nl,lhg->nhg", chooser, down_table)
    own_up = jnp.einsum("l,lhg->hg", own_pick, up_table)
    own_down = jnp.einsum("l,lhg->hg", own_pick, down_table)
    row_index = jnp.arange(hidden_blocks, dtype=jnp.int32)[None, :, None]
    send_up = up_weight[row_index, up_wanted]
    send_down = down_weight[row_index, down_wanted]
    got_up = lax.all_to_all(send_up, "dp", split_axis=0, concat_axis=3, tiled=True)
    got_down = None
    up_local = got_up[0].reshape(hidden_blocks, runs, block_side, block_side)
    chosen = normed.reshape(frames, feat_blocks, block_side)[:, own_up]
    before = jnp.einsum("thgi,hgij->thj", chosen, up_local, preferred_element_type=jnp.float32)
    active = jax.nn.silu(before).astype(jnp.bfloat16)
    got_down = lax.all_to_all(send_down, "dp", split_axis=0, concat_axis=3, tiled=True)
    down_local = got_down[0].reshape(hidden_blocks, runs, block_side, block_side)
    pieces = []
    for run_at in range(runs):
        contrib = jnp.einsum(
            "thi,hij->thj", active, down_local[:, run_at], preferred_element_type=jnp.float32
        )
        targets = run_at * GROUP + jnp.arange(GROUP, dtype=jnp.int32)
        onehot = (own_down[:, run_at, None] == targets).astype(jnp.float32)
        pieces.append(jnp.einsum("thj,hk->tkj", contrib, onehot, precision=lax.Precision.HIGHEST))
    partial_value = jnp.concatenate(pieces, axis=1).reshape(frames, feat_blocks * block_side)
    feedfwd = lax.psum_scatter(
        partial_value.astype(jnp.bfloat16), "tensor", scatter_dimension=1, tiled=True
    ).astype(jnp.float32)
    valid = (jnp.arange(frames, dtype=jnp.int32) < lengths[0]).astype(jnp.float32)
    return ((acoustic.astype(jnp.float32) + feedfwd) * valid[:, None]).astype(jnp.bfloat16)


def solution(mesh):
    in_specs = (
        P(("parts", "dp"), "tensor"),
        P(),
        P("tensor", None, "dp"),
        P("tensor", None, "dp"),
        P(None, "tensor", None),
        P(None, "tensor", None),
        P(("parts", "dp")),
        P(("parts", "dp")),
    )
    out_specs = P(("parts", "dp"), "tensor")
    dp = mesh.shape["dp"]
    rows = BLK // dp
    whole_tiles = mesh.shape["tensor"] == 2 and dp & (dp - 1) == 0 and dp > 1 and rows % 16 == 0
    body = functools.partial(split_body, dp=dp) if whole_tiles else exchange_body
    return jax.shard_map(body, mesh=mesh, in_specs=in_specs, out_specs=out_specs, check_vma=False)
```

```python
import functools

import jax
import jax.numpy as jnp
from jax import lax
from jax.experimental import pallas as pl
from jax.experimental.pallas import tpu as pltpu
from jax.sharding import PartitionSpec as P

BLK = 128
HALF = BLK // 2
GROUP = 8
HSTEP = 16
CHUNKS = 2


def kept_within(keep_mask):
    nlangs, hidden_blocks, feat_blocks = keep_mask.shape
    runs = feat_blocks // GROUP
    picks = jnp.arange(GROUP, dtype=jnp.int32)
    return jnp.sum(keep_mask.reshape(nlangs, hidden_blocks, runs, GROUP) * picks, axis=-1)


def kept_index(keep_mask):
    within = kept_within(keep_mask)
    return within + jnp.arange(within.shape[-1], dtype=jnp.int32) * GROUP


def low_lanes(shape):
    return lax.broadcasted_iota(jnp.int32, shape, len(shape) - 1) < HALF


def half_turn(value):
    return pltpu.roll(value, HALF, value.ndim - 1)


def norm_kernel(side, own_ref, peer_ref, gain_ref, near_ref, far_ref):
    frames, features = own_ref.shape
    slots = features // BLK

    def square(ref):
        total = jnp.zeros((frames, BLK), jnp.float32)
        for d in range(slots):
            wide = ref[:, d * BLK:(d + 1) * BLK].astype(jnp.float32)
            total = total + wide * wide
        return total

    mean = jnp.sum(square(own_ref) + square(peer_ref), axis=-1, keepdims=True) / (2 * features)
    scale = lax.rsqrt(mean + 1e-06)
    low = low_lanes((frames, BLK))
    near_low = low == (side[0] == 0)
    for at, ref in enumerate((own_ref, peer_ref)):
        for d in range(0, slots, 2):
            far = []
            for e in (d, d + 1):
                lanes = slice(e * BLK, (e + 1) * BLK)
                gain = gain_ref[at, :, lanes]
                rounded = (ref[:, lanes].astype(jnp.float32) * scale * gain).astype(jnp.bfloat16).astype(jnp.float32)
                turned = half_turn(rounded)
                near_ref[at * slots + e] = jnp.where(near_low, rounded, turned).astype(jnp.bfloat16)
                far.append(jnp.where(near_low, turned, rounded))
            if at == 0:
                far_ref[d // 2] = jnp.where(low, far[0], far[1]).astype(jnp.bfloat16)


def norm_parts(side, own, peer, gains):
    frames, features = own.shape
    slots = 2 * features // BLK
    return pl.pallas_call(
        norm_kernel,
        grid_spec=pltpu.PrefetchScalarGridSpec(
            num_scalar_prefetch=1,
            grid=(1,),
            in_specs=[
                pl.BlockSpec((frames, features), lambda i, *_: (0, 0)),
                pl.BlockSpec((frames, features), lambda i, *_: (0, 0)),
                pl.BlockSpec((2, 1, features), lambda i, *_: (0, 0, 0)),
            ],
            out_specs=[
                pl.BlockSpec((slots, frames, BLK), lambda i, *_: (0, 0, 0)),
                pl.BlockSpec((slots // 4, frames, BLK), lambda i, *_: (0, 0, 0)),
            ],
        ),
        out_shape=[
            pltpu.HBM((slots, frames, BLK), jnp.bfloat16),
            pltpu.HBM((slots // 4, frames, BLK), jnp.bfloat16),
        ],
        name="norm_parts",
    )(side, own, peer, gains)


def pick_kernel(place, wanted, weight_ref, *refs, rows, runs, base, up, after):
    out_refs, spread = refs[after:-1], refs[-1]
    step = pl.program_id(0) + base
    for h in range(HSTEP):
        for row in range(rows):
            tile = weight_ref[h, :, row * BLK:(row + 1) * BLK].astype(jnp.float32)
            for g in range(runs):
                spread[h * runs + g, row * GROUP:(row + 1) * GROUP, :] = tile[g * GROUP:(g + 1) * GROUP]
    for member in range(wanted.shape[0] // 2):
        pair = 2 * member if up else 2 * (place[0] ^ member)
        for u in range(2):
            for h in range(HSTEP):
                for g in range(runs):
                    at = wanted[pair + u, (step * HSTEP + h) * runs + g]
                    block = spread[h * runs + g, pl.ds(at, rows, stride=GROUP), :]
                    if up and h % 2:
                        block = half_turn(block)
                    block = block.astype(jnp.bfloat16)
                    if up:
                        out_refs[member][u, h, g] = block
                    else:
                        out_refs[u][member, h, g] = block


def pick_blocks(weight, place, wanted, first, count, up, after=()):
    _, feat_blocks, width = weight.shape
    rows = width // BLK
    runs = feat_blocks // GROUP
    base = first // HSTEP
    members = wanted.shape[0] // 2
    outs, lead = (members, 2) if up else (2, members)
    return pl.pallas_call(
        functools.partial(pick_kernel, rows=rows, runs=runs, base=base, up=up, after=len(after)),
        grid_spec=pltpu.PrefetchScalarGridSpec(
            num_scalar_prefetch=2,
            grid=(count // HSTEP,),
            in_specs=[pl.BlockSpec((HSTEP, feat_blocks, width), lambda i, *_: (i + base, 0, 0))]
            + [corner(value) for value in after],
            out_specs=[pl.BlockSpec((lead, HSTEP, runs, rows, BLK), lambda i, *_: (0, i, 0, 0, 0))] * outs,
            scratch_shapes=[pltpu.VMEM((HSTEP * runs, rows * GROUP, BLK), jnp.float32)],
        ),
        out_shape=[pltpu.HBM((lead, count, runs, rows, BLK), jnp.bfloat16)] * outs,
        compiler_params=pltpu.CompilerParams(vmem_limit_bytes=48 << 20),
        name="pick_up" if up else "pick_down",
    )(place, wanted, *in_hbm([weight]), *after)


def corner(value):
    zeros = (0,) * value.ndim
    return pl.BlockSpec((1,) * (value.ndim - 2) + (16, BLK), lambda i, *_: zeros)


def gate_kernel(*refs):
    del refs


def gate(values, after):
    anywhere = pl.BlockSpec(memory_space=pl.ANY)
    return pl.pallas_call(
        gate_kernel,
        grid=(1,),
        in_specs=[anywhere] * len(values) + [corner(value) for value in after],
        out_specs=[anywhere] * len(values),
        out_shape=[pltpu.HBM(value.shape, value.dtype) for value in values],
        input_output_aliases={i: i for i in range(len(values))},
        name="gate",
    )(*in_hbm(values), *after)


def up_kernel(side, place, slots, own_ref, far_a_ref, far_b_ref, *refs, runs, rows):
    weight_refs, refs = refs[:-6], refs[-6:]
    kept_refs, sent_refs, partner, held = refs[:2], refs[2:4], refs[4], refs[5]
    step = pl.program_id(0)
    frames = own_ref.shape[1]
    low = low_lanes((frames, BLK))
    even = low == (side[0] == 0)
    side_rows = rows * len(weight_refs)

    @pl.when(step == 0)
    def _():
        for at, far_ref in enumerate((far_a_ref, far_b_ref)):
            for m in range(far_ref.shape[0]):
                pair = far_ref[m].astype(jnp.float32)
                turned = half_turn(pair)
                first = 2 * (at * far_ref.shape[0] + m)
                partner[first] = jnp.where(low, pair, turned).astype(jnp.bfloat16)
                partner[first + 1] = jnp.where(low, turned, pair).astype(jnp.bfloat16)

    for k, ref in enumerate(weight_refs):
        start = pl.multiple_of(place[k] * rows, rows)
        for u in range(2):
            for h in range(HSTEP):
                for g in range(runs):
                    held[u, h, pl.ds(start + g * side_rows, rows), :] = ref[u, h, g]
    for m in range(HSTEP // 2):
        for u, source in enumerate((own_ref, partner)):
            pair = []
            for h in (2 * m, 2 * m + 1):
                at = [slots[u, (step * HSTEP + h) * runs + g] for g in range(runs)]
                left = jnp.concatenate(
                    [jnp.where(low, source[at[g]], source[at[g + 1]]) for g in range(0, runs, 2)], axis=1
                )
                pair.append(jnp.dot(left, held[u, h], preferred_element_type=jnp.float32))
            kept_refs[u][m] = jnp.where(even, pair[0], pair[1])
            sent_refs[u][m] = jnp.where(even, pair[1], pair[0]).astype(jnp.bfloat16)


def up_project(side, place, slots, own, far, weights):
    _, hidden_blocks, runs, rows, _ = weights[0].shape
    slots_all, frames, _ = own.shape
    out_spec = pl.BlockSpec((HSTEP // 2, frames, BLK), lambda i, *_: (i, 0, 0))
    return pl.pallas_call(
        functools.partial(up_kernel, runs=runs, rows=rows),
        grid_spec=pltpu.PrefetchScalarGridSpec(
            num_scalar_prefetch=3,
            grid=(hidden_blocks // HSTEP,),
            in_specs=[
                pl.BlockSpec((slots_all, frames, BLK), lambda i, *_: (0, 0, 0)),
                pl.BlockSpec((slots_all // 4, frames, BLK), lambda i, *_: (0, 0, 0)),
                pl.BlockSpec((slots_all // 4, frames, BLK), lambda i, *_: (0, 0, 0)),
            ]
            + [pl.BlockSpec((2, HSTEP, runs, rows, BLK), lambda i, *_: (0, i, 0, 0, 0))] * len(weights),
            out_specs=[out_spec] * 4,
            scratch_shapes=[
                pltpu.VMEM((slots_all, frames, BLK), jnp.bfloat16),
                pltpu.VMEM((2, HSTEP, runs * rows * len(weights), BLK), jnp.bfloat16),
            ],
        ),
        out_shape=[pltpu.HBM((hidden_blocks // 2, frames, BLK), jnp.float32)] * 2
        + [pltpu.HBM((hidden_blocks // 2, frames, BLK), jnp.bfloat16)] * 2,
        compiler_params=pltpu.CompilerParams(vmem_limit_bytes=48 << 20),
        name="up_project",
    )(side, place, slots, own, *far, *weights)


def down_kernel(side, which, wanted, *refs, utt, parts, runs, rows):
    refs = list(refs)
    step = pl.program_id(0)
    if parts:
        kept_refs, got_refs, refs = refs[:parts], refs[parts:2 * parts], refs[2 * parts:]
        weight_ref, out_ref, active_ref, held, total = refs
        per_part = pl.num_programs(0) // parts
        for p in range(parts):
            @pl.when(step // per_part == p)
            def _():
                before = kept_refs[p][...] + got_refs[p][...].astype(jnp.float32)
                active_ref[...] = (before / (1.0 + jnp.exp(-before))).astype(jnp.bfloat16)
    else:
        active_ref, weight_ref, out_ref, held, total = refs

    @pl.when(step == 0)
    def _():
        total[...] = jnp.zeros_like(total)
        held[...] = jnp.zeros_like(held)

    for h in range(HSTEP):
        top = HALF * (side[0] ^ (h % 2))
        for member in range(weight_ref.shape[0]):
            start = pl.multiple_of(member * rows + top, rows)
            for g in range(runs):
                at = (h % 2) * runs + g
                held[h // 2, pl.ds(start, rows), at * BLK:(at + 1) * BLK] = weight_ref[member, h, g]
    all_runs = 2 * runs
    for m in range(HSTEP // 2):
        product = jnp.dot(active_ref[m], held[m], preferred_element_type=jnp.float32)
        for odd in range(2):
            for g in range(runs):
                h = step * HSTEP + 2 * m + odd
                at = g * GROUP + wanted[utt, h * all_runs + which[0] * runs + g]
                lane = (odd * runs + g) * BLK
                total[at] += product[:, lane:lane + BLK]

    @pl.when(step == pl.num_programs(0) - 1)
    def _():
        out_ref[...] = total[...].astype(out_ref.dtype)


def down_project(side, which, wanted, sources, weights, utt, out_dtype):
    members, hidden_blocks, all_runs, rows, _ = weights.shape
    runs = all_runs // 2
    outs = runs * GROUP
    frames = sources[-1].shape[1]
    parts = len(sources) // 2
    steps = hidden_blocks // HSTEP
    per_part = steps // max(parts, 1)
    half_step = HSTEP // 2
    active_spec = pl.BlockSpec((half_step, frames, BLK), lambda i, *_: (i, 0, 0))
    if parts:
        source_specs = [
            pl.BlockSpec(
                (half_step, frames, BLK), lambda i, *_, p=p: (jnp.clip(i - p * per_part, 0, per_part - 1), 0, 0)
            )
            for p in range(parts)
        ] * 2
    else:
        source_specs = [active_spec]
    out_specs = [pl.BlockSpec((outs, frames, BLK), lambda i, *_: (0, 0, 0))]
    out_shape = [pltpu.HBM((outs, frames, BLK), out_dtype)]
    if parts:
        out_specs.append(active_spec)
        out_shape.append(pltpu.HBM((hidden_blocks // 2, frames, BLK), jnp.bfloat16))
    return pl.pallas_call(
        functools.partial(down_kernel, utt=utt, parts=parts, runs=runs, rows=rows),
        grid_spec=pltpu.PrefetchScalarGridSpec(
            num_scalar_prefetch=3,
            grid=(steps,),
            in_specs=source_specs
            + [
                pl.BlockSpec((members, HSTEP, runs, rows, BLK), lambda i, side, which, *_: (0, i, which[0], 0, 0))
            ],
            out_specs=out_specs,
            scratch_shapes=[
                pltpu.VMEM((half_step, BLK, 2 * runs * BLK), jnp.bfloat16),
                pltpu.VMEM((outs, frames, BLK), jnp.float32),
            ],
        ),
        out_shape=out_shape,
        compiler_params=pltpu.CompilerParams(vmem_limit_bytes=48 << 20),
        name=f"down_{utt}",
    )(side, which, wanted, *in_hbm(sources[:-parts] if parts else sources), *sources[len(sources) - parts:], weights)


def swap(value, axis, size, step):
    return lax.ppermute(value, axis, [(i, i ^ step) for i in range(size)])


def in_hbm(values):
    return [pltpu.with_memory_space_constraint(value, pltpu.HBM) for value in values]


def split_body(acoustic, norm_gain, up_weight, down_weight, up_keep, down_keep, language, lengths, *, dp):
    frames, features = acoustic.shape
    nlangs, hidden_blocks, feat_blocks = up_keep.shape
    runs = feat_blocks // GROUP
    across = dp // 2
    members = list(range(across))
    here = lax.axis_index("dp").astype(jnp.int32)
    core = lax.axis_index("tensor").astype(jnp.int32)
    side = (here // across)[None]

    peer = swap(acoustic, "tensor", 2, 1)
    gains = norm_gain.reshape(2, 1, features)
    gains = jnp.where(core == 0, gains, gains[::-1])
    near, own_far = norm_parts(side, acoustic, peer, gains)
    far = swap(own_far, "dp", dp, across)
    far = (far, swap(far, "tensor", 2, 1))
    langs = jnp.concatenate([language, swap(language, "dp", dp, across)])
    (langs,) = gate([langs], in_hbm([own_far]))
    step = 1
    while step != across:
        langs = jnp.concatenate([langs, swap(langs, "dp", dp, step)])
        step = 2 * step
    chooser = (langs[:, None] == jnp.arange(nlangs, dtype=jnp.int32)).astype(jnp.int32)
    wanted_up = jnp.einsum("nl,lhg->nhg", chooser, kept_within(up_keep))
    wanted_down = jnp.einsum("nl,lhg->nhg", chooser, kept_within(down_keep))
    up_own = wanted_up[:2] + jnp.arange(runs, dtype=jnp.int32) * GROUP
    slots = (up_own ^ (core * (feat_blocks // 2))).reshape(2, -1)
    wanted_up = wanted_up.reshape(2 * across, -1)
    wanted_down = wanted_down.reshape(2 * across, -1)
    place = jnp.stack([(here ^ k) % across for k in members])

    groups = [[start + k for k in members] for start in (0, across)]

    def by_distance(blocks):
        return [blocks[0]] + [swap(blocks[k], "dp", dp, k) for k in members[1:]]

    def in_order(blocks):
        return lax.all_to_all(blocks, "dp", split_axis=0, concat_axis=0, axis_index_groups=groups, tiled=True)

    count = hidden_blocks // CHUNKS
    kept, crossed, after = ([], []), ([], []), in_hbm([own_far])
    for c in range(CHUNKS):
        blocks = pick_blocks(up_weight, place, wanted_up, c * count, count, True, after)
        after = [*in_hbm(blocks[:1]), far[0]]
        got = by_distance(blocks)
        span = slice(c * count * runs, (c + 1) * count * runs)
        kept_own, kept_far, sent_own, sent_far = up_project(side, place, slots[:, span], near, far, got)
        got_far = swap(sent_own, "dp", dp, across)
        got_own = swap(sent_far, "dp", dp, across)
        for u, (mine, theirs) in enumerate(((kept_own, got_own), (kept_far, got_far))):
            kept[u].append(mine)
            crossed[u].append(theirs)
    own_blocks, far_blocks = pick_blocks(
        down_weight, place, wanted_down, 0, hidden_blocks, False, in_hbm(kept[0][:1])
    )
    (far_blocks,) = gate([far_blocks], [*crossed[1][:1], *got[1:]])
    far_down = in_order(far_blocks)
    (own_blocks,) = gate([own_blocks], [far_down, crossed[1][-1], crossed[0][0]])
    own_down = in_order(own_blocks)
    rows_down = wanted_down[:2]

    def down(which, sources, weights, utt, dtype):
        return down_project(side, which, rows_down, sources, weights, utt, dtype)

    other_core = (1 - core)[None]
    this_core = core[None]
    for_peer, active_far = down(other_core, kept[1] + crossed[1], far_down, 1, jnp.bfloat16)
    from_peer = swap(for_peer, "tensor", 2, 1)
    (far_mine,) = down(this_core, [active_far], far_down, 1, jnp.float32)
    for_side = (far_mine + from_peer.astype(jnp.float32)).astype(jnp.bfloat16)
    from_side = swap(for_side, "dp", dp, across)
    own_peer, active_own = down(other_core, kept[0] + crossed[0], own_down, 0, jnp.bfloat16)
    from_core = swap(own_peer, "tensor", 2, 1)
    (own_mine,) = down(this_core, [active_own], own_down, 0, jnp.float32)
    feedfwd = own_mine + from_core.astype(jnp.float32) + from_side.astype(jnp.float32)
    feedfwd = feedfwd.transpose(1, 0, 2).reshape(frames, features)
    valid = jnp.arange(frames, dtype=jnp.int32)[:, None] < lengths[0]
    return jnp.where(valid, acoustic.astype(jnp.float32) + feedfwd, 0.0).astype(jnp.bfloat16)


def exchange_body(acoustic, norm_gain, up_weight, down_weight, up_keep, down_keep, language, lengths):
    frames = acoustic.shape[0]
    nlangs, hidden_blocks, feat_blocks = up_keep.shape
    block_side = BLK
    runs = feat_blocks // GROUP
    whole = lax.all_gather(acoustic, "tensor", axis=1, tiled=True)
    widened = whole.astype(jnp.float32)
    scale = lax.rsqrt(jnp.mean(widened * widened, axis=-1, keepdims=True) + 1e-06)
    normed = (widened * scale * norm_gain).astype(jnp.bfloat16)
    languages = lax.all_gather(language, "dp", axis=0, tiled=True)
    chooser = (languages[:, None] == jnp.arange(nlangs, dtype=jnp.int32)).astype(jnp.int32)
    own_pick = (language[0] == jnp.arange(nlangs, dtype=jnp.int32)).astype(jnp.int32)
    up_table = kept_index(up_keep)
    down_table = kept_index(down_keep)
    up_wanted = jnp.einsum("nl,lhg->nhg", chooser, up_table)
    down_wanted = jnp.einsum("nl,lhg->nhg", chooser, down_table)
    own_up = jnp.einsum("l,lhg->hg", own_pick, up_table)
    own_down = jnp.einsum("l,lhg->hg", own_pick, down_table)
    row_index = jnp.arange(hidden_blocks, dtype=jnp.int32)[None, :, None]
    send_up = up_weight[row_index, up_wanted]
    send_down = down_weight[row_index, down_wanted]
    got_up = lax.all_to_all(send_up, "dp", split_axis=0, concat_axis=3, tiled=True)
    got_down = None
    up_local = got_up[0].reshape(hidden_blocks, runs, block_side, block_side)
    chosen = normed.reshape(frames, feat_blocks, block_side)[:, own_up]
    before = jnp.einsum("thgi,hgij->thj", chosen, up_local, preferred_element_type=jnp.float32)
    active = jax.nn.silu(before).astype(jnp.bfloat16)
    got_down = lax.all_to_all(send_down, "dp", split_axis=0, concat_axis=3, tiled=True)
    down_local = got_down[0].reshape(hidden_blocks, runs, block_side, block_side)
    pieces = []
    for run_at in range(runs):
        contrib = jnp.einsum(
            "thi,hij->thj", active, down_local[:, run_at], preferred_element_type=jnp.float32
        )
        targets = run_at * GROUP + jnp.arange(GROUP, dtype=jnp.int32)
        onehot = (own_down[:, run_at, None] == targets).astype(jnp.float32)
        pieces.append(jnp.einsum("thj,hk->tkj", contrib, onehot, precision=lax.Precision.HIGHEST))
    partial_value = jnp.concatenate(pieces, axis=1).reshape(frames, feat_blocks * block_side)
    feedfwd = lax.psum_scatter(
        partial_value.astype(jnp.bfloat16), "tensor", scatter_dimension=1, tiled=True
    ).astype(jnp.float32)
    valid = (jnp.arange(frames, dtype=jnp.int32) < lengths[0]).astype(jnp.float32)
    return ((acoustic.astype(jnp.float32) + feedfwd) * valid[:, None]).astype(jnp.bfloat16)


def solution(mesh):
    in_specs = (
        P(("parts", "dp"), "tensor"),
        P(),
        P("tensor", None, "dp"),
        P("tensor", None, "dp"),
        P(None, "tensor", None),
        P(None, "tensor", None),
        P(("parts", "dp")),
        P(("parts", "dp")),
    )
    out_specs = P(("parts", "dp"), "tensor")
    dp = mesh.shape["dp"]
    rows = BLK // dp
    whole_tiles = mesh.shape["tensor"] == 2 and dp & (dp - 1) == 0 and dp > 1 and rows % 16 == 0
    body = functools.partial(split_body, dp=dp) if whole_tiles else exchange_body
    return jax.shard_map(body, mesh=mesh, in_specs=in_specs, out_specs=out_specs, check_vma=False)
```
